32 devices in a mesh: gx: 4 (over y, x), gy: 8 (over z, core).
Axes of the slice: x: 2, y: 2, z: 4, core: 2. Of those that a mesh axis runs over, the one named last changes fastest.
Arguments:
- component_concentration: float32 [64, 32, 3072], P(None, 'gx', 'gy'), may hold values from 0.3 to 3
- thermal_level: float32 [32, 3072], P('gx', 'gy'), may hold values from 0.7 to 2.5
- motion_vector: float32 [3, 32, 3072], P(None, 'gx', 'gy'), may hold values from -6 to 6
- component_weight_per_mole: float32 [64], replicated, may hold values from 0.3 to 3
- collision_size_third: float32 [64, 64], replicated, may hold values from 0.5 to 2
- potential_depth_volume: float32 [64, 64], replicated, may hold values from 0.5 to 4
- binary_drag_logpoly: float32 [4, 64, 64], replicated, may hold values from -0.15 to 2, as said below
- specific_warmth_intercept: float32 [64], replicated, may hold values from 3 to 8
- specific_warmth_gradient: float32 [64], replicated, may hold values from 0 to 1
- component_threshold_stress: float32 [64], replicated, may hold values from 0.5 to 2
Outputs:
- component_concentration_next: float32 [64, 32, 3072], P(None, 'gx', 'gy')
- motion_vector_next: float32 [3, 32, 3072], P(None, 'gx', 'gy')
- thermal_level_next: float32 [32, 3072], P('gx', 'gy')
- friction_limited_interval: float32 [], replicated
The draws below stay inside these ranges and needn't reach their ends.
Inputs may be any that keep to these rules, and one draw needn't show every extreme that they name: `binary_drag_logpoly`: the first of the 4 coefficient matrices lies in 0.5 to 2, the others in -0.15 to 0.15.
All inputs are finite; a program needn't handle non-finite values.
Results may differ from the reference program's by a relative error of at most 0.0003.
Values sent between devices are 32-bit elements; how exact they have to be, the bound alone decides.
No kernel may reach another device: no remote copies, remote signals or barrier semaphores. Data moves between devices by JAX's collectives and lax.ppermute only.
A program may use at most 64 MiB of HBM per device.

```python
import math
import jax
import jax.numpy as jnp
from jax import lax

CHEMICAL_KINDS = 64
TERMS = 4
CX = 8
LATERAL_ZONES = 16
AXIAL_ZONES = 32
NORMAL_ZONES = 192
N_GX = 4


def draw_binary_drag_logpoly(key, part):
    first_key, second_key = jax.random.split(jax.random.fold_in(key, 11))
    leading = jnp.exp(jax.random.uniform(first_key, (1, CHEMICAL_KINDS, CHEMICAL_KINDS), jnp.float32, jnp.log(0.5), jnp.log(2.0)))
    higher = jax.random.uniform(second_key, (TERMS - 1, CHEMICAL_KINDS, CHEMICAL_KINDS), jnp.float32, -0.15, 0.15)
    return jnp.concatenate([leading, higher], axis=0)


def block_levels(rng, extent, cuts, least, largest):
    gain = 1.0
    for dim, parts in cuts:
        steps = jax.random.uniform(jax.random.fold_in(jax.random.fold_in(rng, 6), dim), (parts,), jnp.float32, least / len(cuts), largest / len(cuts))
        gain = gain * jnp.repeat(jnp.exp(steps), extent[dim] // parts).reshape((-1,) + (1,) * (len(extent) - 1 - dim))
    return gain


def gaussian(rng, dims, width, most, shards=(), kind=jnp.bfloat16):
    result = width * jax.random.normal(rng, dims, jnp.float32)
    if shards:
        result = result * block_levels(rng, dims, shards, -0.22, 0.18)
    return jnp.clip(result, -most, most).astype(kind)


def setup_inputs(seed: int = 0) -> dict:
    arg_keys = jax.random.split(jax.random.key(seed), 11)
    return {
        "component_concentration": jnp.clip(jnp.exp(math.log(3.0) - 2.3025851 * jax.random.uniform(arg_keys[0], (CHEMICAL_KINDS, AXIAL_ZONES, NORMAL_ZONES * LATERAL_ZONES), jnp.float32) ** block_levels(arg_keys[0], (CHEMICAL_KINDS, AXIAL_ZONES, NORMAL_ZONES * LATERAL_ZONES), ((1, 4), (2, 8)), -0.2, 0.2)), 0.3, 3.0),
        "thermal_level": jnp.clip(0.7 + 1.8 * jax.random.uniform(arg_keys[1], (AXIAL_ZONES, NORMAL_ZONES * LATERAL_ZONES), jnp.float32) ** block_levels(arg_keys[1], (AXIAL_ZONES, NORMAL_ZONES * LATERAL_ZONES), ((0, 4), (1, 8)), -0.2, 0.2), 0.7, 2.5),
        "motion_vector": gaussian(arg_keys[2], (3, AXIAL_ZONES, NORMAL_ZONES * LATERAL_ZONES), 1.0, 6.0, ((1, 4), (2, 8)), jnp.float32),
        "component_weight_per_mole": jnp.clip(jnp.exp(jax.random.uniform(arg_keys[3], (CHEMICAL_KINDS,), jnp.float32, math.log(0.3), math.log(3.0))), 0.3, 3.0),
        "collision_size_third": jnp.clip(jnp.exp(jax.random.uniform(arg_keys[4], (CHEMICAL_KINDS, CHEMICAL_KINDS), jnp.float32, math.log(0.5), math.log(2.0))), 0.5, 2.0),
        "potential_depth_volume": jnp.clip(jnp.exp(jax.random.uniform(arg_keys[5], (CHEMICAL_KINDS, CHEMICAL_KINDS), jnp.float32, math.log(0.5), math.log(4.0))), 0.5, 4.0),
        "binary_drag_logpoly": draw_binary_drag_logpoly(jax.random.fold_in(arg_keys[10], 71), 0),
        "specific_warmth_intercept": jnp.clip(jnp.exp(jax.random.uniform(arg_keys[7], (CHEMICAL_KINDS,), jnp.float32, math.log(3.0), math.log(8.0))), 3.0, 8.0),
        "specific_warmth_gradient": jnp.clip(jax.random.uniform(arg_keys[8], (CHEMICAL_KINDS,), jnp.float32, 0.0, 1.0), 0.0, 1.0),
        "component_threshold_stress": jnp.clip(jnp.exp(jax.random.uniform(arg_keys[9], (CHEMICAL_KINDS,), jnp.float32, math.log(0.5), math.log(2.0))), 0.5, 2.0),
    }


HIGHEST = lax.Precision.HIGHEST
CFL_NUMBER = 0.12
GAS_SCALE = 0.01
BETA = 0.7862

def mixture(fluid_snapshot, tables):
    component_weight_per_mole, collision_size_third, potential_depth_volume, binary_drag_logpoly, specific_warmth_intercept, specific_warmth_gradient, component_threshold_stress = tables
    species = component_weight_per_mole.shape[0]
    cell_shape = fluid_snapshot.shape[1:]
    flattened = fluid_snapshot.reshape(fluid_snapshot.shape[0], -1)
    partial_mass = flattened[:species]
    temper = flattened[species]
    mixture_density = lax.optimization_barrier(jnp.sum(partial_mass, axis=0))
    fraction = partial_mass / mixture_density
    mole_count = fraction / component_weight_per_mole[:, None]
    mole_total = lax.optimization_barrier(jnp.sum(mole_count, axis=0))
    molefr = mole_count / mole_total
    mean_mass = 1.0 / mole_total
    size_mix = lax.optimization_barrier(jnp.sum(molefr * jnp.dot(collision_size_third, molefr, precision=HIGHEST, preferred_element_type=jnp.float32), axis=0))
    energy_mix = lax.optimization_barrier(jnp.sum(molefr * jnp.dot(potential_depth_volume, molefr, precision=HIGHEST, preferred_element_type=jnp.float32), axis=0)) / size_mix
    reduced = temper / energy_mix
    collision = 1.16145 * reduced ** (-0.14874) + 0.52487 * jnp.exp(-0.7732 * reduced) + 2.16178 * jnp.exp(-2.43787 * reduced)
    viscosity = 40.785 * (0.809 * 0.809) * jnp.sqrt(mean_mass * temper) / (size_mix ** (2.0 / 3.0) * collision)
    heat_molar = lax.optimization_barrier(jnp.sum(molefr * (specific_warmth_intercept[:, None] + specific_warmth_gradient[:, None] * temper), axis=0))
    excess = heat_molar - 2.5
    zeta_term = 2.0 + 10.5 * (reduced / 1.2593) ** 2
    psi_term = 1.0 + excess * (0.215 + 0.28288 * excess - 1.061 * BETA + 0.26665 * zeta_term) / (0.6366 + BETA * zeta_term + 1.061 * excess * BETA)
    conduct = 7.452 * viscosity * psi_term / mean_mass
    mass_heat_capacity = heat_molar / mean_mass
    pressure = GAS_SCALE * mixture_density * temper / mean_mass
    critical = lax.optimization_barrier(jnp.sum(molefr * component_threshold_stress[:, None], axis=0))
    takahashi = 1.0 / (1.0 + 0.25 * (pressure / critical) ** 2)
    logtemp = jnp.log(temper)
    row_index = lax.broadcasted_iota(jnp.int32, (species, species), 0)
    col_index = lax.broadcasted_iota(jnp.int32, (species, species), 1)
    off_diagonal = jnp.where(row_index == col_index, 0.0, 1.0).astype(jnp.float32)
    resist = jnp.zeros_like(molefr)
    powers = jnp.ones_like(temper)
    for order in range(binary_drag_logpoly.shape[0]):
        resist = resist + powers * jnp.dot(binary_drag_logpoly[order] * off_diagonal, molefr, precision=HIGHEST, preferred_element_type=jnp.float32)
        powers = powers * logtemp
    diffusive = takahashi * (1.0 - fraction) * temper * jnp.sqrt(temper) / (pressure * resist)
    carried = mixture_density * diffusive
    rate_max = jnp.maximum(jnp.maximum(viscosity / mixture_density, conduct / (mixture_density * mass_heat_capacity)), lax.optimization_barrier(jnp.max(diffusive, axis=0)))
    packed = jnp.concatenate([carried, viscosity[None], conduct[None]], axis=0).reshape((species + 2,) + cell_shape)
    return (packed, mass_heat_capacity.reshape(cell_shape), rate_max.reshape(cell_shape))

def face_pair(source, axis_dim, cell_count):
    pieces = [lax.slice_in_dim(source, offset, offset + cell_count + 1, axis=axis_dim) for offset in range(4)]
    face_value = (9.0 * (pieces[1] + pieces[2]) - (pieces[0] + pieces[3])) / 16.0
    face_slope = (27.0 * (pieces[2] - pieces[1]) - (pieces[3] - pieces[0])) / 24.0
    return (face_value, face_slope)

def differ(through, axis_dim, cell_count):
    return lax.slice_in_dim(through, 1, cell_count + 1, axis=axis_dim) - lax.slice_in_dim(through, 0, cell_count, axis=axis_dim)

def line_rates(state_line, packed_line, axis_dim, cell_count):
    species = packed_line.shape[0] - 2
    partial_mass = state_line[:species]
    mixture_density = lax.optimization_barrier(jnp.sum(partial_mass, axis=0, keepdims=True))
    fraction = partial_mass / mixture_density
    frac_value, frac_slope = face_pair(fraction, axis_dim, cell_count)
    carried_value = face_pair(packed_line[:species], axis_dim, cell_count)[0]
    drift = lax.optimization_barrier(jnp.sum(carried_value * frac_slope, axis=0, keepdims=True))
    species_rate = differ(carried_value * frac_slope - frac_value * drift, axis_dim, cell_count)
    visc_value = face_pair(packed_line[species:species + 1], axis_dim, cell_count)[0]
    motion_slope = face_pair(state_line[species + 1:], axis_dim, cell_count)[1]
    momentum = differ(visc_value * motion_slope, axis_dim, cell_count)
    cond_value = face_pair(packed_line[species + 1:], axis_dim, cell_count)[0]
    temp_slope = face_pair(state_line[species:species + 1], axis_dim, cell_count)[1]
    thermal_power_source = differ(cond_value * temp_slope, axis_dim, cell_count)
    return (species_rate, momentum, thermal_power_source)

def join_blocks(stacked):
    moved = jnp.moveaxis(stacked, 0, 1)
    return moved.reshape(stacked.shape[1], AXIAL_ZONES, NORMAL_ZONES * LATERAL_ZONES)

def reference(component_concentration, thermal_level, motion_vector, component_weight_per_mole, collision_size_third, potential_depth_volume, binary_drag_logpoly, specific_warmth_intercept, specific_warmth_gradient, component_threshold_stress):
    tables = (component_weight_per_mole, collision_size_third, potential_depth_volume, binary_drag_logpoly, specific_warmth_intercept, specific_warmth_gradient, component_threshold_stress)
    fluid_snapshot = jnp.concatenate([component_concentration, thermal_level[None], motion_vector], axis=0).reshape(CHEMICAL_KINDS + 4, AXIAL_ZONES, NORMAL_ZONES, LATERAL_ZONES)

    def block(index):
        rows_x = jnp.clip(index * CX - 2 + jnp.arange(CX + 4, dtype=jnp.int32), 0, AXIAL_ZONES - 1).astype(jnp.int32)
        slab = jnp.take(fluid_snapshot, rows_x, axis=1)
        slab = jnp.pad(slab, ((0, 0), (0, 0), (2, 2), (2, 2)), mode='wrap')
        packed, mass_heat_capacity, rate_max = mixture(slab, tables)
        x_part = line_rates(slab[:, :, 2:-2, 2:-2], packed[:, :, 2:-2, 2:-2], 1, CX)
        y_part = line_rates(slab[:, 2:-2, :, 2:-2], packed[:, 2:-2, :, 2:-2], 2, NORMAL_ZONES)
        z_part = line_rates(slab[:, 2:-2, 2:-2, :], packed[:, 2:-2, 2:-2, :], 3, LATERAL_ZONES)
        species_rate = x_part[0] + y_part[0] + z_part[0]
        momentum = x_part[1] + y_part[1] + z_part[1]
        thermal_power_source = x_part[2] + y_part[2] + z_part[2]
        mixture_density = lax.optimization_barrier(jnp.sum(slab[:CHEMICAL_KINDS, 2:-2, 2:-2, 2:-2], axis=0))
        core_heat = mass_heat_capacity[2:-2, 2:-2, 2:-2]
        return (species_rate, momentum / mixture_density, thermal_power_source[0] / (mixture_density * core_heat), jnp.max(rate_max[2:-2, 2:-2, 2:-2]))
    outcome = lax.map(block, jnp.arange(N_GX, dtype=jnp.int32))
    species_rate = join_blocks(outcome[0])
    momentum = join_blocks(outcome[1])
    thermal_power_source = outcome[2].reshape(AXIAL_ZONES, NORMAL_ZONES * LATERAL_ZONES)
    friction_limited_interval = CFL_NUMBER / jnp.max(outcome[3])
    component_concentration_next = component_concentration + friction_limited_interval * species_rate
    motion_vector_next = motion_vector + friction_limited_interval * momentum
    thermal_level_next = thermal_level + friction_limited_interval * thermal_power_source
    return (component_concentration_next, motion_vector_next, thermal_level_next, friction_limited_interval)
```

```python
import functools

import jax
import jax.numpy as jnp
from jax import lax
from jax.experimental import pallas as pl
from jax.experimental.pallas import tpu as pltpu
from jax.sharding import PartitionSpec as P

LATERAL_ZONES = 16
CFL_NUMBER = 0.12
GAS_SCALE = 0.01
BETA = 0.7862
LANES = 128
EXTRA = 8
F32 = jnp.float32
VMEM = pltpu.MemorySpace.VMEM


def row_ids():
    return lax.broadcasted_iota(jnp.int32, (EXTRA, LANES), 0)


def lane_ids():
    return lax.broadcasted_iota(jnp.int32, (8, LANES), 1)


def split(value):
    high = value.astype(jnp.bfloat16)
    low = (value - high.astype(F32)).astype(jnp.bfloat16)
    return high, low


def fold_rows(value, op):
    parts = [value[8 * i : 8 * i + 8] for i in range(value.shape[0] // 8)]
    while len(parts) > 1:
        half = [op(parts[i], parts[i + 1]) for i in range(0, len(parts) - 1, 2)]
        parts = half + ([parts[-1]] if len(parts) % 2 else [])
    return parts[0]


def column_sum(value):
    return jnp.sum(fold_rows(value, jnp.add), axis=0, keepdims=True)


def write_matrix(mass_ref, size_ref, energy_ref, poly_ref, base_ref, slope_ref, crit_ref, mat_ref):
    species = mass_ref.shape[1]
    terms = poly_ref.shape[0] // species
    inverse = 1.0 / mass_ref[...]
    rows = lax.broadcasted_iota(jnp.int32, (species, species), 0)
    cols = lax.broadcasted_iota(jnp.int32, (species, species), 1)
    same = rows == cols
    column = jnp.sum(
        jnp.where(same, jnp.broadcast_to(inverse, (species, species)), 0.0), axis=1, keepdims=True
    )

    def put(start, block):
        high, low = split(block)
        high, low = high.astype(F32), low.astype(F32)
        mat_ref[start : start + block.shape[0], :] = jnp.concatenate(
            [high, high, low], axis=1
        ).astype(jnp.bfloat16)

    for k in range(terms):
        block = jnp.where(same, 0.0, poly_ref[k * species : (k + 1) * species, :])
        put(k * species, block * inverse)
    put(terms * species, size_ref[...] * inverse * column)
    put((terms + 1) * species, energy_ref[...] * inverse * column)
    lin = lax.broadcasted_iota(jnp.int32, (16, species), 0)
    block = jnp.where(lin == 0, 1.0, 0.0)
    for k, row in enumerate(
        (inverse, base_ref[...] * inverse, slope_ref[...] * inverse, crit_ref[...] * inverse)
    ):
        block = jnp.where(lin == k + 1, row, block)
    put((terms + 2) * species, block)


def mix_products(units, group, read, mat_ref, lin_ref, resist_ref, extra=None):
    ids = row_ids()

    def step(j, carry):
        pieces = [read(j, i) for i in range(group)]
        mass = [p[0] for p in pieces]
        species = mass[0].shape[0]
        terms = mat_ref.shape[0] // species - 2
        wide = jnp.concatenate(mass, axis=1)
        high, low = split(wide)
        stacked = jnp.concatenate([high, low, high], axis=0)
        product = jnp.dot(mat_ref[...], stacked, preferred_element_type=F32)
        for i, (m, temper) in enumerate(pieces):
            part = product[:, i * LANES : (i + 1) * LANES]
            u = j * group + i
            logt = jnp.log(temper)
            total = part[(terms - 1) * species : terms * species]
            for k in range(terms - 2, -1, -1):
                total = total * logt + part[k * species : (k + 1) * species]
            resist_ref[u, 0:species, :] = total
            size = column_sum(m * part[terms * species : (terms + 1) * species])
            energy = column_sum(m * part[(terms + 1) * species : (terms + 2) * species])
            lin = part[(terms + 2) * species : (terms + 2) * species + 8]
            lin = jnp.where(ids == 5, size, jnp.where(ids == 6, energy, lin))
            lin = jnp.where(ids == 7, temper, lin)
            lin_ref[pl.ds(pl.multiple_of(u * 8, 8), 8), :] = lin
            if extra is not None:
                extra(j, i, u, temper, part[(terms + 2) * species : (terms + 2) * species + 1])
        return carry

    lax.fori_loop(0, units // group, step, 0)


def mix_cells(units, lin_ref, plane_ref):
    def plane(k):
        return lin_ref[pl.ds(k, units, stride=8), :]

    density, moles, base, slope, crit, size, energy, temper = [plane(k) for k in range(8)]
    reduced = temper * size / energy
    collision = (
        1.16145 * jnp.exp(-0.14874 * jnp.log(reduced))
        + 0.52487 * jnp.exp(-0.7732 * reduced)
        + 2.16178 * jnp.exp(-2.43787 * reduced)
    )
    inv_moles = 1.0 / moles
    mean_mass = density * inv_moles
    size_mix = size * inv_moles * inv_moles
    viscosity = (
        (40.785 * (0.809 * 0.809))
        * jnp.sqrt(mean_mass * temper)
        / (jnp.exp((2.0 / 3.0) * jnp.log(size_mix)) * collision)
    )
    heat_total = base + slope * temper
    excess = heat_total * inv_moles - 2.5
    ratio = reduced * (1.0 / 1.2593)
    zeta = 2.0 + 10.5 * ratio * ratio
    psi = 1.0 + excess * (0.215 + 0.28288 * excess - 1.061 * BETA + 0.26665 * zeta) / (
        0.6366 + BETA * zeta + (1.061 * BETA) * excess
    )
    conduct = 7.452 * viscosity * psi / mean_mass
    over = GAS_SCALE * temper * moles * moles / crit
    takahashi = 1.0 / (1.0 + 0.25 * over * over)
    front = density * takahashi * jnp.sqrt(temper) * (1.0 / GAS_SCALE)
    inv_density = 1.0 / density
    inv_heat = 1.0 / heat_total
    plane_ref[0] = front
    plane_ref[1] = inv_density
    plane_ref[2] = viscosity
    plane_ref[3] = conduct
    plane_ref[4] = inv_heat
    return jnp.maximum(viscosity * inv_density, conduct * inv_heat)


def coefficient_rows(plane_ref, u):
    ids = row_ids()
    visc = plane_ref[2, pl.ds(u, 1), :]
    cond = plane_ref[3, pl.ds(u, 1), :]
    return jnp.where(ids == 0, cond, jnp.where(ids < 4, visc, 0.0))


def mix_halo(units, group, state_ref, mat_ref, lin_ref, plane_ref, carried_ref):
    species = state_ref.shape[1] - EXTRA

    def read(j, i):
        u = j * group + i
        density = state_ref[u, species + 4 : species + 5, :]
        return state_ref[u, 0:species, :] * density, state_ref[u, species : species + 1, :]

    mix_products(units, group, read, mat_ref, lin_ref, carried_ref)
    mix_cells(units, lin_ref, plane_ref)

    def step(u, carry):
        front = plane_ref[0, pl.ds(u, 1), :]
        fraction = state_ref[u, 0:species, :]
        carried_ref[u, 0:species, :] = front * ((1.0 - fraction) / carried_ref[u, 0:species, :])
        carried_ref[u, species : species + EXTRA, :] = coefficient_rows(plane_ref, u)
        return carry

    lax.fori_loop(0, units, step, 0)


def mixture_kernel(
    conc_hbm, temper_ref, motion_ref, mass_ref, size_ref, energy_ref, poly_ref, base_ref,
    slope_ref, crit_ref,
    state_ref, carried_ref, inverse_ref, mat_ref, first_x, second_x, first_y, second_y, rate_ref,
    conc_ref, lin_ref, plane_ref, other_ref, sem,
):
    tiles, _, _ = conc_ref.shape
    width = temper_ref.shape[0]
    species = mass_ref.shape[1]
    units = tiles * width
    copies = [
        pltpu.make_async_copy(
            conc_hbm.at[:, pl.ds(t * LANES, LANES)], conc_ref.at[t], sem.at[t]
        )
        for t in range(tiles)
    ]
    for c in copies:
        c.start()
    write_matrix(
        mass_ref, size_ref, energy_ref, poly_ref, base_ref, slope_ref, crit_ref, mat_ref
    )
    for t in range(tiles):
        ls = slice(t * LANES, (t + 1) * LANES)
        other_ref[t, 0:width, :] = temper_ref[:, ls]
        other_ref[t, width : 4 * width, :] = motion_ref[:, ls]
    for c in copies:
        c.wait()
    ids = row_ids()

    def read(x, t):
        mass = conc_ref[t, pl.ds(x, species, stride=width), :]
        return mass, other_ref[t, pl.ds(x, 1), :]

    def extra(x, t, u, temper, density):
        block = jnp.where(ids == 0, temper, jnp.where(ids == 4, density, 0.0))
        for c in range(3):
            row = other_ref[t, pl.ds((c + 1) * width + x, 1), :]
            block = jnp.where(ids == c + 1, row, block)
        state_ref[u, species : species + EXTRA, :] = block

    mix_products(units, tiles, read, mat_ref, lin_ref, carried_ref, extra)
    rates = mix_cells(units, lin_ref, plane_ref)

    def step(x, best):
        for t in range(tiles):
            u = x * tiles + t
            front = plane_ref[0, pl.ds(u, 1), :]
            inv_density = plane_ref[1, pl.ds(u, 1), :]
            fraction = conc_ref[t, pl.ds(x, species, stride=width), :] * inv_density
            share = (1.0 - fraction) / carried_ref[u, 0:species, :]
            state_ref[u, 0:species, :] = fraction
            carried_ref[u, 0:species, :] = front * share
            carried_ref[u, species : species + EXTRA, :] = coefficient_rows(plane_ref, u)
            inv_heat = plane_ref[4, pl.ds(u, 1), :]
            inverse_ref[u] = jnp.where(ids == 0, inv_heat, jnp.where(ids < 4, inv_density, 0.0))
            best = jnp.maximum(best, fold_rows(share, jnp.maximum) * (front * inv_density))
        return best

    best = lax.fori_loop(0, width, step, jnp.zeros((8, LANES), F32))
    top = jnp.maximum(jnp.max(best), jnp.max(rates))
    rate_ref[...] = jnp.full(rate_ref.shape, top, F32)

    even_x = lax.rem(lax.axis_index("gx"), 2) == 0
    upper = (width - 2) * tiles
    start_a = jnp.where(even_x, upper, 0)
    start_b = upper - start_a
    for k in range(2 * tiles):
        first_x[k] = state_ref[start_a + k]
        second_x[k] = state_ref[start_b + k]
    even_y = lax.rem(lax.axis_index("gy"), 2) == 0
    reach = 2 * LATERAL_ZONES
    per = LANES // reach
    lanes = lax.broadcasted_iota(jnp.int32, (species + EXTRA, LANES), 1)
    for g in range(width // per):
        low = high = None
        for k in range(per):
            x = g * per + k
            bottom = state_ref[x * tiles]
            ceiling = state_ref[x * tiles + tiles - 1]
            if k > 0:
                bottom = pltpu.roll(bottom, k * reach, 1)
            if k < per - 1:
                ceiling = pltpu.roll(ceiling, (k + 1) * reach, 1)
            if k == 0:
                low, high = bottom, ceiling
            else:
                low = jnp.where(lanes >= k * reach, bottom, low)
                high = jnp.where(lanes >= k * reach, ceiling, high)
        first_y[g] = jnp.where(even_y, high, low)
        second_y[g] = jnp.where(even_y, low, high)


def weigh(before, here, after, beyond):
    value = 9.0 * (here + after) - (before + beyond)
    slope = 27.0 * (after - here) - (beyond - before)
    return value, slope


def only_value(before, here, after, beyond):
    return 9.0 * (here + after) - (before + beyond)


def cross_kernel(
    state_ref, carried_ref, mat_ref, first_ref, second_ref,
    rate_ref,
    halo_ref, halo_carried, wrap_ref, wrap_carried, lin_ref, plane_ref, prod_ref, value_ref,
):
    units, rows, _ = state_ref.shape
    species = rows - EXTRA
    packs = first_ref.shape[0]
    zc = LATERAL_ZONES
    reach = 2 * zc
    per = LANES // reach
    width = packs * per
    tiles = units // width
    even_y = lax.rem(lax.axis_index("gy"), 2) == 0
    for g in range(packs):
        a, b = first_ref[g], second_ref[g]
        halo_ref[g] = jnp.where(even_y, a, b)
        halo_ref[packs + g] = jnp.where(even_y, b, a)
    mix_halo(2 * packs, 2 * packs, halo_ref, mat_ref, lin_ref, plane_ref, halo_carried)
    wide = lax.broadcasted_iota(jnp.int32, (rows, LANES), 1)
    for x in range(width):
        g, k = divmod(x, per)
        for src, dst in ((halo_ref, wrap_ref), (halo_carried, wrap_carried)):
            above, below = src[g], src[packs + g]
            if k > 0:
                above = pltpu.roll(above, LANES - k * reach, 1)
            if k < per - 1:
                below = pltpu.roll(below, LANES - (k + 1) * reach, 1)
            dst[x] = jnp.where(wide < LANES - reach, above, below)

    lane = lane_ids()
    chunks = rows // 8
    last = species // 8

    def y_shift(parts, amount):
        turned = [pltpu.roll(p, (LANES - amount) % LANES, 1) for p in parts]
        n = len(parts)
        if amount > 0:
            return [
                jnp.where(lane < LANES - amount, turned[t], turned[(t + 1) % n]) for t in range(n)
            ]
        return [jnp.where(lane >= -amount, turned[t], turned[t - 1]) for t in range(n)]

    z_index = lane % zc

    def z_shift(part, amount):
        near = pltpu.roll(part, (LANES - amount) % LANES, 1)
        far = pltpu.roll(part, (zc - amount) if amount > 0 else LANES - (zc + amount), 1)
        if amount > 0:
            return jnp.where(z_index < zc - amount, near, far)
        return jnp.where(z_index >= -amount, near, far)

    def step(x, carry):
        drift_y = [None] * (tiles + 1)
        drift_z = [None] * tiles
        for c in range(chunks):
            rs = slice(8 * c, 8 * c + 8)
            f = [state_ref[x * tiles + t, rs, :] for t in range(tiles)]
            h = [carried_ref[x * tiles + t, rs, :] for t in range(tiles)]
            fy, hy = f + [wrap_ref[x, rs, :]], h + [wrap_carried[x, rs, :]]
            fs = [y_shift(fy, a) for a in (-zc, zc, 2 * zc)]
            hs = [y_shift(hy, a) for a in (-zc, zc, 2 * zc)]
            for t in range(tiles + 1):
                v, s = weigh(fs[0][t], fy[t], fs[1][t], fs[2][t])
                p = only_value(hs[0][t], hy[t], hs[1][t], hs[2][t]) * s
                prod_ref[t, rs, :] = p
                value_ref[t, rs, :] = v
                if c < last:
                    drift_y[t] = p if c == 0 else drift_y[t] + p
            for t in range(tiles):
                v, s = weigh(z_shift(f[t], -1), f[t], z_shift(f[t], 1), z_shift(f[t], 2))
                p = only_value(z_shift(h[t], -1), h[t], z_shift(h[t], 1), z_shift(h[t], 2)) * s
                prod_ref[tiles + 1 + t, rs, :] = p
                value_ref[tiles + 1 + t, rs, :] = v
                if c < last:
                    drift_z[t] = p if c == 0 else drift_z[t] + p
        drift_y = [jnp.sum(d, axis=0, keepdims=True) * 0.0625 for d in drift_y]
        drift_z = [jnp.sum(d, axis=0, keepdims=True) * 0.0625 for d in drift_z]
        for c in range(chunks):
            rs = slice(8 * c, 8 * c + 8)

            def flux(slot, drift):
                p = prod_ref[slot, rs, :]
                return p - value_ref[slot, rs, :] * drift if c < last else p

            fy = [flux(t, drift_y[t]) for t in range(tiles + 1)]
            back = y_shift(fy, -zc)
            for t in range(tiles):
                fz = flux(tiles + 1 + t, drift_z[t])
                rate_ref[x * tiles + t, rs, :] = (fy[t] - back[t]) + (fz - z_shift(fz, -1))
        return carry

    lax.fori_loop(0, width, step, 0)


def stream_kernel(
    state_ref, carried_ref, mat_ref, first_ref, second_ref, partial_ref, inverse_ref,
    species_ref, others_ref,
    halo_ref, halo_carried, lin_ref, plane_ref,
):
    units, rows, _ = state_ref.shape
    species = rows - EXTRA
    half = first_ref.shape[0]
    tiles = half // 2
    width = units // tiles
    me, peers = lax.axis_index("gx"), lax.axis_size("gx")
    even_x = lax.rem(me, 2) == 0
    at_start, at_end = me == 0, me == peers - 1

    for k in range(half):
        a, b = first_ref[k], second_ref[k]
        low = jnp.where(even_x, b, a)
        high = jnp.where(even_x, a, b)
        halo_ref[k] = jnp.where(at_start, state_ref[k % tiles], low)
        halo_ref[half + k] = jnp.where(at_end, state_ref[units - tiles + k % tiles], high)
    mix_halo(2 * half, tiles, halo_ref, mat_ref, lin_ref, plane_ref, halo_carried)

    def step(t, carry):
        def row(inner, outer, x):
            if x < 0:
                return outer[(x + 2) * tiles + t]
            if x >= width:
                return outer[half + (x - width) * tiles + t]
            return inner[x * tiles + t]

        before = None
        for face in range(width + 1):
            f = [row(state_ref, halo_ref, face + k) for k in (-2, -1, 0, 1)]
            h = [row(carried_ref, halo_carried, face + k) for k in (-2, -1, 0, 1)]
            value, slope = weigh(*f)
            product = only_value(*h) * slope
            drift = column_sum(product[:species]) * 0.0625
            flux = jnp.concatenate(
                [product[:species] - value[:species] * drift, product[species:]], axis=0
            )
            if face > 0:
                x = face - 1
                u = x * tiles + t
                total = (flux - before) + partial_ref[u]
                species_ref[t, pl.ds(x, species, stride=width), :] = total[:species]
                others_ref[t, pl.ds(x, EXTRA, stride=width), :] = total[species:] * inverse_ref[u]
            before = flux
        return carry

    lax.fori_loop(0, tiles, step, 0)


def finish_kernel(
    conc_ref, temper_ref, motion_ref, species_ref, others_ref, top_ref,
    conc_out, temper_out, motion_out, interval_out,
):
    tiles = species_ref.shape[0]
    width = temper_ref.shape[0]
    fastest = jnp.max(top_ref[...], axis=0)
    interval = CFL_NUMBER / jnp.max(fastest, axis=(0, 1), keepdims=True)
    interval_out[...] = interval
    factor = interval * (1.0 / 384.0)
    for t in range(tiles):
        ls = slice(t * LANES, (t + 1) * LANES)
        conc_out[:, ls] = conc_ref[:, ls] + factor * species_ref[t]
        temper_out[:, ls] = temper_ref[:, ls] + factor * others_ref[t, 0:width, :]
        motion_out[:, ls] = motion_ref[:, ls] + factor * others_ref[t, width : 4 * width, :]


def call(kernel, name, outs, ins, scratch=()):
    return pl.pallas_call(
        kernel,
        out_shape=[jax.ShapeDtypeStruct(s, d) for s, d in outs],
        in_specs=[pl.BlockSpec(memory_space=m) for m in ins],
        out_specs=[pl.BlockSpec(memory_space=VMEM) for _ in outs],
        scratch_shapes=list(scratch),
        name=name,
    )


def body(
    component_concentration,
    thermal_level,
    motion_vector,
    component_weight_per_mole,
    collision_size_third,
    potential_depth_volume,
    binary_drag_logpoly,
    specific_warmth_intercept,
    specific_warmth_gradient,
    component_threshold_stress,
):
    species, width, line = component_concentration.shape
    terms = binary_drag_logpoly.shape[0]
    tiles = line // LANES
    units = width * tiles
    rows = species + EXTRA
    per = LANES // (2 * LATERAL_ZONES)
    packs = width // per
    nx, ny = lax.axis_size("gx"), lax.axis_size("gy")
    devices = nx * ny
    conc = component_concentration.reshape(species * width, line)
    motion = motion_vector.reshape(3 * width, line)
    mat_rows = (terms + 2) * species + 16
    mix_scratch = lambda n: [pltpu.VMEM((n * 8, LANES), F32), pltpu.VMEM((5, n, LANES), F32)]
    state, carried, inverse, mat, first_x, second_x, first_y, second_y, rate = call(
        mixture_kernel,
        "mixture",
        [
            ((units, rows, LANES), F32),
            ((units, rows, LANES), F32),
            ((units, EXTRA, LANES), F32),
            ((mat_rows, 3 * species), jnp.bfloat16),
            ((2 * tiles, rows, LANES), F32),
            ((2 * tiles, rows, LANES), F32),
            ((packs, rows, LANES), F32),
            ((packs, rows, LANES), F32),
            ((devices, 8, LANES), F32),
        ],
        [pl.ANY] + [VMEM] * 9,
        [pltpu.VMEM((tiles, species * width, LANES), F32)]
        + mix_scratch(units)
        + [pltpu.VMEM((tiles, 4 * width, LANES), F32)]
        + [pltpu.SemaphoreType.DMA((tiles,))],
    )(
        conc,
        thermal_level,
        motion,
        component_weight_per_mole[None],
        collision_size_third,
        potential_depth_volume,
        binary_drag_logpoly.reshape(terms * species, species),
        specific_warmth_intercept[None],
        specific_warmth_gradient[None],
        component_threshold_stress[None],
    )
    top = lax.all_to_all(rate, ("gx", "gy"), 0, 0, tiled=True)
    pair_first = lambda n: [(i, i ^ 1) for i in range(n)]
    pair_second = lambda n: [(i, (i + 1) % n if i % 2 else (i - 1) % n) for i in range(n)]
    inside = [(i, j) for i, j in pair_second(nx) if abs(i - j) == 1]
    got_first_x = lax.ppermute(first_x, "gx", pair_first(nx))
    got_second_x = lax.ppermute(second_x, "gx", inside)
    got_first_y = lax.ppermute(first_y, "gy", pair_first(ny))
    got_second_y = lax.ppermute(second_y, "gy", pair_second(ny))
    (cross,) = call(
        cross_kernel,
        "cross",
        [((units, rows, LANES), F32)],
        [VMEM] * 5,
        [
            pltpu.VMEM((2 * packs, rows, LANES), F32),
            pltpu.VMEM((2 * packs, rows, LANES), F32),
            pltpu.VMEM((width, rows, LANES), F32),
            pltpu.VMEM((width, rows, LANES), F32),
        ]
        + mix_scratch(2 * packs)
        + [pltpu.VMEM((2 * tiles + 1, rows, LANES), F32)] * 2,
    )(state, carried, mat, got_first_y, got_second_y)
    species_rate, other_rate = call(
        stream_kernel,
        "stream",
        [((tiles, species * width, LANES), F32), ((tiles, EXTRA * width, LANES), F32)],
        [VMEM] * 7,
        [
            pltpu.VMEM((4 * tiles, rows, LANES), F32),
            pltpu.VMEM((4 * tiles, rows, LANES), F32),
        ]
        + mix_scratch(4 * tiles),
    )(state, carried, mat, got_first_x, got_second_x, cross, inverse)
    conc_next, temper_next, motion_next, interval = call(
        finish_kernel,
        "finish",
        [
            (conc.shape, F32),
            (thermal_level.shape, F32),
            (motion.shape, F32),
            ((1, 1), F32),
        ],
        [VMEM] * 6,
    )(conc, thermal_level, motion, species_rate, other_rate, top)
    return (
        conc_next.reshape(component_concentration.shape),
        motion_next.reshape(motion_vector.shape),
        temper_next,
        interval.reshape(()),
    )


def solution(mesh):
    in_specs = (
        P(None, "gx", "gy"),
        P("gx", "gy"),
        P(None, "gx", "gy"),
    ) + (P(),) * 7
    out_specs = (P(None, "gx", "gy"), P(None, "gx", "gy"), P("gx", "gy"), P())
    return jax.shard_map(body, mesh=mesh, in_specs=in_specs, out_specs=out_specs, check_vma=False)
```

```python
import functools

import jax
import jax.numpy as jnp
from jax import lax
from jax.experimental import pallas as pl
from jax.experimental.pallas import tpu as pltpu
from jax.sharding import PartitionSpec as P

LATERAL_ZONES = 16
CFL_NUMBER = 0.12
GAS_SCALE = 0.01
BETA = 0.7862
LANES = 128
EXTRA = 8
F32 = jnp.float32
VMEM = pltpu.MemorySpace.VMEM


def row_ids():
    return lax.broadcasted_iota(jnp.int32, (EXTRA, LANES), 0)


def lane_ids():
    return lax.broadcasted_iota(jnp.int32, (8, LANES), 1)


def split(value):
    high = value.astype(jnp.bfloat16)
    low = (value - high.astype(F32)).astype(jnp.bfloat16)
    return high, low


def fold_rows(value, op):
    parts = [value[8 * i : 8 * i + 8] for i in range(value.shape[0] // 8)]
    while len(parts) > 1:
        half = [op(parts[i], parts[i + 1]) for i in range(0, len(parts) - 1, 2)]
        parts = half + ([parts[-1]] if len(parts) % 2 else [])
    return parts[0]


def column_sum(value):
    return jnp.sum(fold_rows(value, jnp.add), axis=0, keepdims=True)


def write_matrix(mass_ref, size_ref, energy_ref, poly_ref, base_ref, slope_ref, crit_ref, mat_ref):
    species = mass_ref.shape[1]
    terms = poly_ref.shape[0] // species
    inverse = 1.0 / mass_ref[...]
    rows = lax.broadcasted_iota(jnp.int32, (species, species), 0)
    cols = lax.broadcasted_iota(jnp.int32, (species, species), 1)
    same = rows == cols
    column = jnp.sum(
        jnp.where(same, jnp.broadcast_to(inverse, (species, species)), 0.0), axis=1, keepdims=True
    )

    def put(start, block):
        high, low = split(block)
        high, low = high.astype(F32), low.astype(F32)
        mat_ref[start : start + block.shape[0], :] = jnp.concatenate(
            [high, high, low], axis=1
        ).astype(jnp.bfloat16)

    for k in range(terms):
        block = jnp.where(same, 0.0, poly_ref[k * species : (k + 1) * species, :])
        put(k * species, block * inverse)
    put(terms * species, size_ref[...] * inverse * column)
    put((terms + 1) * species, energy_ref[...] * inverse * column)
    lin = lax.broadcasted_iota(jnp.int32, (16, species), 0)
    block = jnp.where(lin == 0, 1.0, 0.0)
    for k, row in enumerate(
        (inverse, base_ref[...] * inverse, slope_ref[...] * inverse, crit_ref[...] * inverse)
    ):
        block = jnp.where(lin == k + 1, row, block)
    put((terms + 2) * species, block)


def mix_products(units, group, read, mat_ref, lin_ref, resist_ref, extra=None):
    ids = row_ids()

    def step(j, carry):
        pieces = [read(j, i) for i in range(group)]
        mass = [p[0] for p in pieces]
        species = mass[0].shape[0]
        terms = mat_ref.shape[0] // species - 2
        wide = jnp.concatenate(mass, axis=1)
        high, low = split(wide)
        stacked = jnp.concatenate([high, low, high], axis=0)
        product = jnp.dot(mat_ref[...], stacked, preferred_element_type=F32)
        for i, (m, temper) in enumerate(pieces):
            part = product[:, i * LANES : (i + 1) * LANES]
            u = j * group + i
            logt = jnp.log(temper)
            total = part[(terms - 1) * species : terms * species]
            for k in range(terms - 2, -1, -1):
                total = total * logt + part[k * species : (k + 1) * species]
            resist_ref[u, 0:species, :] = total
            size = column_sum(m * part[terms * species : (terms + 1) * species])
            energy = column_sum(m * part[(terms + 1) * species : (terms + 2) * species])
            lin = part[(terms + 2) * species : (terms + 2) * species + 8]
            lin = jnp.where(ids == 5, size, jnp.where(ids == 6, energy, lin))
            lin = jnp.where(ids == 7, temper, lin)
            lin_ref[pl.ds(pl.multiple_of(u * 8, 8), 8), :] = lin
            if extra is not None:
                extra(j, i, u, temper, part[(terms + 2) * species : (terms + 2) * species + 1])
        return carry

    lax.fori_loop(0, units // group, step, 0)


def mix_cells(units, lin_ref, plane_ref):
    def plane(k):
        return lin_ref[pl.ds(k, units, stride=8), :]

    density, moles, base, slope, crit, size, energy, temper = [plane(k) for k in range(8)]
    reduced = temper * size / energy
    collision = (
        1.16145 * jnp.exp(-0.14874 * jnp.log(reduced))
        + 0.52487 * jnp.exp(-0.7732 * reduced)
        + 2.16178 * jnp.exp(-2.43787 * reduced)
    )
    inv_moles = 1.0 / moles
    mean_mass = density * inv_moles
    size_mix = size * inv_moles * inv_moles
    viscosity = (
        (40.785 * (0.809 * 0.809))
        * jnp.sqrt(mean_mass * temper)
        / (jnp.exp((2.0 / 3.0) * jnp.log(size_mix)) * collision)
    )
    heat_total = base + slope * temper
    excess = heat_total * inv_moles - 2.5
    ratio = reduced * (1.0 / 1.2593)
    zeta = 2.0 + 10.5 * ratio * ratio
    psi = 1.0 + excess * (0.215 + 0.28288 * excess - 1.061 * BETA + 0.26665 * zeta) / (
        0.6366 + BETA * zeta + (1.061 * BETA) * excess
    )
    conduct = 7.452 * viscosity * psi / mean_mass
    over = GAS_SCALE * temper * moles * moles / crit
    takahashi = 1.0 / (1.0 + 0.25 * over * over)
    front = density * takahashi * jnp.sqrt(temper) * (1.0 / GAS_SCALE)
    inv_density = 1.0 / density
    inv_heat = 1.0 / heat_total
    plane_ref[0] = front
    plane_ref[1] = inv_density
    plane_ref[2] = viscosity
    plane_ref[3] = conduct
    plane_ref[4] = inv_heat
    return jnp.maximum(viscosity * inv_density, conduct * inv_heat)


def coefficient_rows(plane_ref, u):
    ids = row_ids()
    visc = plane_ref[2, pl.ds(u, 1), :]
    cond = plane_ref[3, pl.ds(u, 1), :]
    return jnp.where(ids == 0, cond, jnp.where(ids < 4, visc, 0.0))


def mix_halo(units, group, state_ref, mat_ref, lin_ref, plane_ref, carried_ref):
    species = state_ref.shape[1] - EXTRA

    def read(j, i):
        u = j * group + i
        density = state_ref[u, species + 4 : species + 5, :]
        return state_ref[u, 0:species, :] * density, state_ref[u, species : species + 1, :]

    mix_products(units, group, read, mat_ref, lin_ref, carried_ref)
    mix_cells(units, lin_ref, plane_ref)

    def step(u, carry):
        front = plane_ref[0, pl.ds(u, 1), :]
        fraction = state_ref[u, 0:species, :]
        carried_ref[u, 0:species, :] = front * ((1.0 - fraction) / carried_ref[u, 0:species, :])
        carried_ref[u, species : species + EXTRA, :] = coefficient_rows(plane_ref, u)
        return carry

    lax.fori_loop(0, units, step, 0)


def mixture_kernel(
    conc_hbm, temper_hbm, motion_hbm, mass_hbm, size_hbm, energy_hbm, poly_hbm, base_hbm,
    slope_hbm, crit_hbm,
    base_ref, state_ref, carried_ref, mat_ref, first_x, second_x, first_y, second_y, rate_ref,
    mass_ref, size_ref, energy_ref, poly_ref, heat_ref, slope_ref, crit_ref, lin_ref, plane_ref,
    table_sem, cell_sem,
):
    tiles = base_ref.shape[0]
    width = temper_hbm.shape[0]
    species = mass_ref.shape[1]
    units = tiles * width
    cells = species * width
    pairs = (
        (mass_hbm, mass_ref), (size_hbm, size_ref), (energy_hbm, energy_ref),
        (poly_hbm, poly_ref), (base_hbm, heat_ref), (slope_hbm, slope_ref), (crit_hbm, crit_ref),
    )
    tables = [
        pltpu.make_async_copy(src, dst, table_sem.at[k]) for k, (src, dst) in enumerate(pairs)
    ]
    copies = []
    for t in range(tiles):
        ls = pl.ds(t * LANES, LANES)
        for k, (src, start) in enumerate(
            ((conc_hbm, 0), (temper_hbm, cells), (motion_hbm, cells + width))
        ):
            dst = base_ref.at[t, pl.ds(start, src.shape[0])]
            copies.append(pltpu.make_async_copy(src.at[:, ls], dst, cell_sem.at[3 * t + k]))
    for c in tables + copies:
        c.start()
    for c in tables:
        c.wait()
    write_matrix(
        mass_ref, size_ref, energy_ref, poly_ref, heat_ref, slope_ref, crit_ref, mat_ref
    )
    for c in copies:
        c.wait()
    ids = row_ids()

    def read(x, t):
        mass = base_ref[t, pl.ds(x, species, stride=width), :]
        return mass, base_ref[t, pl.ds(cells + x, 1), :]

    def extra(x, t, u, temper, density):
        block = jnp.where(ids == 0, temper, jnp.where(ids == 4, density, 0.0))
        for c in range(3):
            row = base_ref[t, pl.ds(cells + (c + 1) * width + x, 1), :]
            block = jnp.where(ids == c + 1, row, block)
        state_ref[u, species : species + EXTRA, :] = block

    mix_products(units, tiles, read, mat_ref, lin_ref, carried_ref, extra)
    rates = mix_cells(units, lin_ref, plane_ref)

    def step(x, best):
        for t in range(tiles):
            u = x * tiles + t
            front = plane_ref[0, pl.ds(u, 1), :]
            inv_density = plane_ref[1, pl.ds(u, 1), :]
            fraction = base_ref[t, pl.ds(x, species, stride=width), :] * inv_density
            share = (1.0 - fraction) / carried_ref[u, 0:species, :]
            state_ref[u, 0:species, :] = fraction
            carried_ref[u, 0:species, :] = front * share
            carried_ref[u, species : species + EXTRA, :] = coefficient_rows(plane_ref, u)
            state_ref[u, species + 5 : species + 6, :] = plane_ref[4, pl.ds(u, 1), :]
            state_ref[u, species + 6 : species + 7, :] = inv_density
            best = jnp.maximum(best, fold_rows(share, jnp.maximum) * (front * inv_density))
        return best

    best = lax.fori_loop(0, width, step, jnp.zeros((8, LANES), F32))
    top = jnp.maximum(jnp.max(best), jnp.max(rates))
    rate_ref[...] = jnp.full(rate_ref.shape, top, F32)

    even_x = lax.rem(lax.axis_index("gx"), 2) == 0
    upper = (width - 2) * tiles
    start_a = jnp.where(even_x, upper, 0)
    start_b = upper - start_a
    for k in range(2 * tiles):
        first_x[k] = state_ref[start_a + k]
        second_x[k] = state_ref[start_b + k]
    even_y = lax.rem(lax.axis_index("gy"), 2) == 0
    reach = 2 * LATERAL_ZONES
    per = LANES // reach
    lanes = lax.broadcasted_iota(jnp.int32, (species + EXTRA, LANES), 1)
    for g in range(width // per):
        low = high = None
        for k in range(per):
            x = g * per + k
            bottom = state_ref[x * tiles]
            ceiling = state_ref[x * tiles + tiles - 1]
            if k > 0:
                bottom = pltpu.roll(bottom, k * reach, 1)
            if k < per - 1:
                ceiling = pltpu.roll(ceiling, (k + 1) * reach, 1)
            if k == 0:
                low, high = bottom, ceiling
            else:
                low = jnp.where(lanes >= k * reach, bottom, low)
                high = jnp.where(lanes >= k * reach, ceiling, high)
        first_y[g] = jnp.where(even_y, high, low)
        second_y[g] = jnp.where(even_y, low, high)


def weigh(before, here, after, beyond):
    value = 9.0 * (here + after) - (before + beyond)
    slope = 27.0 * (after - here) - (beyond - before)
    return value, slope


def only_value(before, here, after, beyond):
    return 9.0 * (here + after) - (before + beyond)


def z_shift(part, amount):
    zc = LATERAL_ZONES
    z_index = lax.broadcasted_iota(jnp.int32, part.shape, 1) % zc
    near = pltpu.roll(part, (LANES - amount) % LANES, 1)
    far = pltpu.roll(part, (zc - amount) if amount > 0 else LANES - (zc + amount), 1)
    if amount > 0:
        return jnp.where(z_index < zc - amount, near, far)
    return jnp.where(z_index >= -amount, near, far)


def span_kernel(group, state_ref, carried_ref, rate_ref, mat_ref):
    units, rows, _ = state_ref.shape
    species = rows - EXTRA
    zc = LATERAL_ZONES
    src = lax.broadcasted_iota(jnp.int32, (LANES, LANES), 0)
    dst = lax.broadcasted_iota(jnp.int32, (LANES, LANES), 1)
    near = (src // zc) == (dst // zc)
    step = jnp.where(near, (src % zc - dst % zc + 1 + zc) % zc, 4)
    value = jnp.where((step == 1) | (step == 2), 9.0, jnp.where((step == 0) | (step == 3), -1.0, 0.0))
    slope = jnp.where(
        step == 2,
        27.0,
        jnp.where(step == 1, -27.0, jnp.where(step == 3, -1.0, jnp.where(step == 0, 1.0, 0.0))),
    )
    for k in range(2):
        rs = slice(k * LANES, (k + 1) * LANES)
        mat_ref[rs, 0:LANES] = value.astype(jnp.bfloat16)
        mat_ref[rs, LANES : 2 * LANES] = slope.astype(jnp.bfloat16)

    def halves(ref, j):
        wide = ref[pl.ds(j * group, group)].reshape(group * rows, LANES)
        return jnp.concatenate(split(wide), axis=1)

    def work(j, carry):
        both = jnp.dot(halves(state_ref, j), mat_ref[...], preferred_element_type=F32)
        front = jnp.dot(
            halves(carried_ref, j), mat_ref[:, 0:LANES], preferred_element_type=F32
        )
        for i in range(group):
            rs = slice(i * rows, (i + 1) * rows)
            product = front[rs] * both[rs, LANES:]
            drift = column_sum(product[:species]) * 0.0625
            flux = jnp.concatenate(
                [product[:species] - both[rs, :LANES][:species] * drift, product[species:]], axis=0
            )
            rate_ref[j * group + i] = flux - z_shift(flux, -1)
        return carry

    lax.fori_loop(0, units // group, work, 0)


def cross_kernel(
    state_ref, carried_ref, mat_ref, first_ref, second_ref, partial_ref,
    rate_ref, mat_out,
    halo_ref, halo_carried, wrap_ref, wrap_carried, lin_ref, plane_ref, prod_ref, value_ref,
):
    mat_out[...] = mat_ref[...]
    units, rows, _ = state_ref.shape
    species = rows - EXTRA
    packs = first_ref.shape[0]
    zc = LATERAL_ZONES
    reach = 2 * zc
    per = LANES // reach
    width = packs * per
    tiles = units // width
    even_y = lax.rem(lax.axis_index("gy"), 2) == 0
    for g in range(packs):
        a, b = first_ref[g], second_ref[g]
        halo_ref[g] = jnp.where(even_y, a, b)
        halo_ref[packs + g] = jnp.where(even_y, b, a)
    mix_halo(2 * packs, 2 * packs, halo_ref, mat_ref, lin_ref, plane_ref, halo_carried)
    wide = lax.broadcasted_iota(jnp.int32, (rows, LANES), 1)
    for x in range(width):
        g, k = divmod(x, per)
        for src, dst in ((halo_ref, wrap_ref), (halo_carried, wrap_carried)):
            above, below = src[g], src[packs + g]
            if k > 0:
                above = pltpu.roll(above, LANES - k * reach, 1)
            if k < per - 1:
                below = pltpu.roll(below, LANES - (k + 1) * reach, 1)
            dst[x] = jnp.where(wide < LANES - reach, above, below)

    lane = lane_ids()
    chunks = rows // 8
    last = species // 8

    def y_shift(parts, amount):
        turned = [pltpu.roll(p, (LANES - amount) % LANES, 1) for p in parts]
        n = len(parts)
        if amount > 0:
            return [
                jnp.where(lane < LANES - amount, turned[t], turned[(t + 1) % n]) for t in range(n)
            ]
        return [jnp.where(lane >= -amount, turned[t], turned[t - 1]) for t in range(n)]

    def step(x, carry):
        drift = [None] * (tiles + 1)
        for c in range(chunks):
            rs = slice(8 * c, 8 * c + 8)
            f = [state_ref[x * tiles + t, rs, :] for t in range(tiles)] + [wrap_ref[x, rs, :]]
            h = [carried_ref[x * tiles + t, rs, :] for t in range(tiles)]
            h = h + [wrap_carried[x, rs, :]]
            fs = [y_shift(f, a) for a in (-zc, zc, 2 * zc)]
            hs = [y_shift(h, a) for a in (-zc, zc, 2 * zc)]
            for t in range(tiles + 1):
                v, s = weigh(fs[0][t], f[t], fs[1][t], fs[2][t])
                p = only_value(hs[0][t], h[t], hs[1][t], hs[2][t]) * s
                prod_ref[t, rs, :] = p
                value_ref[t, rs, :] = v
                if c < last:
                    drift[t] = p if c == 0 else drift[t] + p
        drift = [jnp.sum(d, axis=0, keepdims=True) * 0.0625 for d in drift]
        for c in range(chunks):
            rs = slice(8 * c, 8 * c + 8)
            flux = [prod_ref[t, rs, :] for t in range(tiles + 1)]
            if c < last:
                flux = [flux[t] - value_ref[t, rs, :] * drift[t] for t in range(tiles + 1)]
            back = y_shift(flux, -zc)
            for t in range(tiles):
                u = x * tiles + t
                rate_ref[u, rs, :] = partial_ref[u, rs, :] + (flux[t] - back[t])
        return carry

    lax.fori_loop(0, width, step, 0)


def stream_kernel(
    state_ref, carried_ref, mat_ref, first_ref, second_ref, partial_ref,
    rate_ref,
    halo_ref, halo_carried, lin_ref, plane_ref,
):
    units, rows, _ = state_ref.shape
    species = rows - EXTRA
    half = first_ref.shape[0]
    tiles = half // 2
    width = units // tiles
    me, peers = lax.axis_index("gx"), lax.axis_size("gx")
    even_x = lax.rem(me, 2) == 0
    at_start, at_end = me == 0, me == peers - 1

    for k in range(half):
        a, b = first_ref[k], second_ref[k]
        low = jnp.where(even_x, b, a)
        high = jnp.where(even_x, a, b)
        halo_ref[k] = jnp.where(at_start, state_ref[k % tiles], low)
        halo_ref[half + k] = jnp.where(at_end, state_ref[units - tiles + k % tiles], high)
    mix_halo(2 * half, tiles, halo_ref, mat_ref, lin_ref, plane_ref, halo_carried)

    ids = row_ids()

    def step(t, carry):
        def row(inner, outer, x):
            if x < 0:
                return outer[(x + 2) * tiles + t]
            if x >= width:
                return outer[half + (x - width) * tiles + t]
            return inner[x * tiles + t]

        before = None
        for face in range(width + 1):
            f = [row(state_ref, halo_ref, face + k) for k in (-2, -1, 0, 1)]
            h = [row(carried_ref, halo_carried, face + k) for k in (-2, -1, 0, 1)]
            value, slope = weigh(*f)
            product = only_value(*h) * slope
            drift = column_sum(product[:species]) * 0.0625
            flux = jnp.concatenate(
                [product[:species] - value[:species] * drift, product[species:]], axis=0
            )
            if face > 0:
                x = face - 1
                u = x * tiles + t
                total = (flux - before) + partial_ref[u]
                inv_heat = state_ref[u, species + 5 : species + 6, :]
                inv_density = state_ref[u, species + 6 : species + 7, :]
                factor = jnp.where(ids == 0, inv_heat, inv_density)
                total = jnp.concatenate([total[:species], total[species:] * factor], axis=0)
                rate_ref[t, pl.ds(x, rows, stride=width), :] = total
            before = flux
        return carry

    lax.fori_loop(0, tiles, step, 0)


def finish_kernel(
    base_ref, rate_ref, top_ref,
    conc_hbm, temper_hbm, motion_hbm, interval_ref,
    next_ref, sem,
):
    tiles, count, _ = base_ref.shape
    fastest = jnp.max(top_ref[...], axis=0)
    interval = CFL_NUMBER / jnp.max(fastest, axis=(0, 1), keepdims=True)
    interval_ref[...] = interval
    factor = interval * (1.0 / 384.0)
    copies = []
    for t in range(tiles):
        next_ref[t] = base_ref[t] + factor * rate_ref[t, 0:count, :]
        ls = pl.ds(t * LANES, LANES)
        start = 0
        for k, dst in enumerate((conc_hbm, temper_hbm, motion_hbm)):
            src = next_ref.at[t, pl.ds(start, dst.shape[0])]
            copy = pltpu.make_async_copy(src, dst.at[:, ls], sem.at[3 * t + k])
            copy.start()
            copies.append(copy)
            start += dst.shape[0]
    for copy in copies:
        copy.wait()


def call(kernel, name, outs, ins, scratch=()):
    shapes, specs = [], []
    for shape, dtype, place in outs:
        shapes.append(
            pltpu.VMEM(shape, dtype) if place is True else jax.ShapeDtypeStruct(shape, dtype)
        )
        specs.append(pl.BlockSpec(memory_space=pl.ANY if place is pl.ANY else VMEM))
    run = pl.pallas_call(
        kernel,
        out_shape=shapes,
        in_specs=[pl.BlockSpec(memory_space=pltpu.HBM if m is pl.ANY else VMEM) for m in ins],
        out_specs=specs,
        scratch_shapes=list(scratch),
        name=name,
        compiler_params=pltpu.CompilerParams(vmem_limit_bytes=16 << 20),
    )

    def apply(*args):
        return run(
            *[
                pltpu.with_memory_space_constraint(a, pltpu.VMEM if m is True else pltpu.HBM)
                for a, m in zip(args, ins)
            ]
        )

    return apply


def body(
    component_concentration,
    thermal_level,
    motion_vector,
    component_weight_per_mole,
    collision_size_third,
    potential_depth_volume,
    binary_drag_logpoly,
    specific_warmth_intercept,
    specific_warmth_gradient,
    component_threshold_stress,
):
    species, width, line = component_concentration.shape
    terms = binary_drag_logpoly.shape[0]
    tiles = line // LANES
    units = width * tiles
    rows = species + EXTRA
    per = LANES // (2 * LATERAL_ZONES)
    packs = width // per
    nx, ny = lax.axis_size("gx"), lax.axis_size("gy")
    devices = nx * ny
    conc = component_concentration.reshape(species * width, line)
    motion = motion_vector.reshape(3 * width, line)
    mat_rows = (terms + 2) * species + 16
    count = (species + 4) * width
    keep = True
    field = ((units, rows, LANES), F32, keep)
    mix_scratch = lambda n: [pltpu.VMEM((n * 8, LANES), F32), pltpu.VMEM((5, n, LANES), F32)]
    base, state, carried, mat, first_x, second_x, first_y, second_y, rate = call(
        mixture_kernel,
        "mixture",
        [
            ((tiles, count, LANES), F32, keep),
            field,
            field,
            ((mat_rows, 3 * species), jnp.bfloat16, keep),
            ((2 * tiles, rows, LANES), F32, keep),
            ((2 * tiles, rows, LANES), F32, keep),
            ((packs, rows, LANES), F32, keep),
            ((packs, rows, LANES), F32, keep),
            ((devices, 8, LANES), F32, keep),
        ],
        [pl.ANY] * 10,
        [
            pltpu.VMEM((1, species), F32),
            pltpu.VMEM((species, species), F32),
            pltpu.VMEM((species, species), F32),
            pltpu.VMEM((terms * species, species), F32),
            pltpu.VMEM((1, species), F32),
            pltpu.VMEM((1, species), F32),
            pltpu.VMEM((1, species), F32),
        ]
        + mix_scratch(units)
        + [pltpu.SemaphoreType.DMA((7,)), pltpu.SemaphoreType.DMA((3 * tiles,))],
    )(
        conc,
        thermal_level,
        motion,
        component_weight_per_mole[None],
        collision_size_third,
        potential_depth_volume,
        binary_drag_logpoly.reshape(terms * species, species),
        specific_warmth_intercept[None],
        specific_warmth_gradient[None],
        component_threshold_stress[None],
    )
    top = lax.all_to_all(rate, ("gx", "gy"), 0, 0, tiled=True)
    pair_first = lambda n: [(i, i ^ 1) for i in range(n)]
    pair_second = lambda n: [(i, (i + 1) % n if i % 2 else (i - 1) % n) for i in range(n)]
    inside = [(i, j) for i, j in pair_second(nx) if abs(i - j) == 1]
    got_first_x = lax.ppermute(first_x, "gx", pair_first(nx))
    got_second_x = lax.ppermute(second_x, "gx", inside)
    got_first_y = lax.ppermute(first_y, "gy", pair_first(ny))
    got_second_y = lax.ppermute(second_y, "gy", pair_second(ny))
    group = 2 * tiles if width % 2 == 0 else tiles
    (span,) = call(
        functools.partial(span_kernel, group),
        "span",
        [field],
        [keep] * 2,
        [pltpu.VMEM((2 * LANES, 2 * LANES), jnp.bfloat16)],
    )(state, carried)
    cross, mat = call(
        cross_kernel,
        "cross",
        [field, ((mat_rows, 3 * species), jnp.bfloat16, keep)],
        [keep] * 6,
        [
            pltpu.VMEM((2 * packs, rows, LANES), F32),
            pltpu.VMEM((2 * packs, rows, LANES), F32),
            pltpu.VMEM((width, rows, LANES), F32),
            pltpu.VMEM((width, rows, LANES), F32),
        ]
        + mix_scratch(2 * packs)
        + [pltpu.VMEM((tiles + 1, rows, LANES), F32)] * 2,
    )(state, carried, mat, got_first_y, got_second_y, span)
    (total,) = call(
        stream_kernel,
        "stream",
        [((tiles, rows * width, LANES), F32, keep)],
        [keep] * 6,
        [
            pltpu.VMEM((4 * tiles, rows, LANES), F32),
            pltpu.VMEM((4 * tiles, rows, LANES), F32),
        ]
        + mix_scratch(4 * tiles),
    )(state, carried, mat, got_first_x, got_second_x, cross)
    conc_next, temper_next, motion_next, interval = call(
        finish_kernel,
        "finish",
        [
            (conc.shape, F32, pl.ANY),
            (thermal_level.shape, F32, pl.ANY),
            (motion.shape, F32, pl.ANY),
            ((1, 1), F32, None),
        ],
        [keep] * 3,
        [pltpu.VMEM((tiles, count, LANES), F32), pltpu.SemaphoreType.DMA((3 * tiles,))],
    )(base, total, top)
    return (
        conc_next.reshape(component_concentration.shape),
        motion_next.reshape(motion_vector.shape),
        temper_next,
        interval.reshape(()),
    )


def solution(mesh):
    in_specs = (
        P(None, "gx", "gy"),
        P("gx", "gy"),
        P(None, "gx", "gy"),
    ) + (P(),) * 7
    out_specs = (P(None, "gx", "gy"), P(None, "gx", "gy"), P("gx", "gy"), P())
    return jax.shard_map(body, mesh=mesh, in_specs=in_specs, out_specs=out_specs, check_vma=False)
```

```python
import functools

import jax
import jax.numpy as jnp
import numpy as np
from jax import lax
from jax.experimental import pallas as pl
from jax.experimental.pallas import tpu as pltpu
from jax.sharding import PartitionSpec as P


LATERAL_ZONES = 16
CFL_NUMBER = 0.12
GAS_SCALE = 0.01
BETA = 0.7862
LANES = 128
EXTRA = 8
F32 = jnp.float32
VMEM = pltpu.MemorySpace.VMEM


def row_ids():
    return lax.broadcasted_iota(jnp.int32, (EXTRA, LANES), 0)


def split(value):
    high = value.astype(jnp.bfloat16)
    low = (value - high.astype(F32)).astype(jnp.bfloat16)
    return high, low


def fold_rows(value, op):
    parts = [value[8 * i : 8 * i + 8] for i in range(value.shape[0] // 8)]
    while len(parts) > 1:
        half = [op(parts[i], parts[i + 1]) for i in range(0, len(parts) - 1, 2)]
        parts = half + ([parts[-1]] if len(parts) % 2 else [])
    return parts[0]


def column_sum(value):
    return jnp.sum(fold_rows(value, jnp.add), axis=0, keepdims=True)


def write_matrix(mass_ref, size_ref, energy_ref, poly_ref, base_ref, slope_ref, crit_ref, mat_ref):
    species = mass_ref.shape[1]
    terms = poly_ref.shape[0] // species
    inverse = 1.0 / mass_ref[...]
    rows = lax.broadcasted_iota(jnp.int32, (species, species), 0)
    cols = lax.broadcasted_iota(jnp.int32, (species, species), 1)
    same = rows == cols
    column = jnp.sum(
        jnp.where(same, jnp.broadcast_to(inverse, (species, species)), 0.0), axis=1, keepdims=True
    )

    def put(start, block):
        high, low = split(block)
        high, low = high.astype(F32), low.astype(F32)
        mat_ref[start : start + block.shape[0], :] = jnp.concatenate(
            [high, low], axis=1
        ).astype(jnp.bfloat16)

    for k in range(terms):
        block = jnp.where(same, 0.0, poly_ref[k * species : (k + 1) * species, :])
        put(k * species, block * inverse)
    put(terms * species, size_ref[...] * inverse * column)
    put((terms + 1) * species, energy_ref[...] * inverse * column)
    lin = lax.broadcasted_iota(jnp.int32, (16, species), 0)
    block = jnp.where(lin == 0, 1.0, 0.0)
    for k, row in enumerate(
        (inverse, base_ref[...] * inverse, slope_ref[...] * inverse, crit_ref[...] * inverse)
    ):
        block = jnp.where(lin == k + 1, row, block)
    put((terms + 2) * species, block)


def mix_products(units, group, read, mat_ref, lin_ref, resist_ref, extra=None):
    ids = row_ids()

    def step(j, carry):
        pieces = [read(j, i) for i in range(group)]
        mass = [p[0] for p in pieces]
        species = mass[0].shape[0]
        terms = mat_ref.shape[0] // species - 2
        wide = jnp.concatenate(mass, axis=1)
        high, low = split(wide)
        stacked = jnp.concatenate([high, high, low, low], axis=0)
        both = jnp.concatenate([mat_ref[...], mat_ref[...]], axis=1)
        product = jnp.dot(both, stacked, preferred_element_type=F32)
        for i, (m, temper) in enumerate(pieces):
            part = product[:, i * LANES : (i + 1) * LANES]
            u = j * group + i
            logt = jnp.log(temper)
            total = part[(terms - 1) * species : terms * species]
            for k in range(terms - 2, -1, -1):
                total = total * logt + part[k * species : (k + 1) * species]
            resist_ref[u, 0:species, :] = total
            size = column_sum(m * part[terms * species : (terms + 1) * species])
            energy = column_sum(m * part[(terms + 1) * species : (terms + 2) * species])
            lin = part[(terms + 2) * species : (terms + 2) * species + 8]
            lin = jnp.where(ids == 5, size, jnp.where(ids == 6, energy, lin))
            lin = jnp.where(ids == 7, temper, lin)
            lin_ref[pl.ds(pl.multiple_of(u * 8, 8), 8), :] = lin
            if extra is not None:
                extra(j, i, u, temper, part[(terms + 2) * species : (terms + 2) * species + 1])
        return carry

    lax.fori_loop(0, units // group, step, 0)


def mix_cells(units, lin_ref, plane_ref):
    def plane(k):
        return lin_ref[pl.ds(k, units, stride=8), :]

    density, moles, base, slope, crit, size, energy, temper = [plane(k) for k in range(8)]
    reduced = temper * size / energy
    collision = (
        1.16145 * jnp.exp(-0.14874 * jnp.log(reduced))
        + 0.52487 * jnp.exp(-0.7732 * reduced)
        + 2.16178 * jnp.exp(-2.43787 * reduced)
    )
    inv_moles = 1.0 / moles
    mean_mass = density * inv_moles
    size_mix = size * inv_moles * inv_moles
    viscosity = (
        (40.785 * (0.809 * 0.809))
        * jnp.sqrt(mean_mass * temper)
        / (jnp.exp((2.0 / 3.0) * jnp.log(size_mix)) * collision)
    )
    heat_total = base + slope * temper
    excess = heat_total * inv_moles - 2.5
    ratio = reduced * (1.0 / 1.2593)
    zeta = 2.0 + 10.5 * ratio * ratio
    psi = 1.0 + excess * (0.215 + 0.28288 * excess - 1.061 * BETA + 0.26665 * zeta) / (
        0.6366 + BETA * zeta + (1.061 * BETA) * excess
    )
    conduct = 7.452 * viscosity * psi / mean_mass
    over = GAS_SCALE * temper * moles * moles / crit
    takahashi = 1.0 / (1.0 + 0.25 * over * over)
    front = density * takahashi * jnp.sqrt(temper) * (1.0 / GAS_SCALE)
    inv_density = 1.0 / density
    inv_heat = 1.0 / heat_total
    plane_ref[0] = front
    plane_ref[1] = inv_density
    plane_ref[2] = viscosity
    plane_ref[3] = conduct
    plane_ref[4] = inv_heat
    return jnp.maximum(viscosity * inv_density, conduct * inv_heat)


def coefficient_rows(plane_ref, u):
    ids = row_ids()
    visc = plane_ref[2, pl.ds(u, 1), :]
    cond = plane_ref[3, pl.ds(u, 1), :]
    return jnp.where(ids == 0, cond, jnp.where(ids < 4, visc, 0.0))


def mix_halo(units, group, state_ref, mat_ref, lin_ref, plane_ref, carried_ref):
    species = state_ref.shape[1] - EXTRA

    def read(j, i):
        u = j * group + i
        density = state_ref[u, species + 4 : species + 5, :]
        return state_ref[u, 0:species, :] * density, state_ref[u, species : species + 1, :]

    mix_products(units, group, read, mat_ref, lin_ref, carried_ref)
    mix_cells(units, lin_ref, plane_ref)

    def step(u, carry):
        front = plane_ref[0, pl.ds(u, 1), :]
        fraction = state_ref[u, 0:species, :]
        carried_ref[u, 0:species, :] = front * ((1.0 - fraction) / carried_ref[u, 0:species, :])
        carried_ref[u, species : species + EXTRA, :] = coefficient_rows(plane_ref, u)
        return carry

    lax.fori_loop(0, units, step, 0)


def pack_cells(ref, unit, tiles, start, per):
    reach = LANES // per
    rows = ref.shape[1]
    lanes = lax.broadcasted_iota(jnp.int32, (rows, LANES), 1)
    out = None
    for k in range(per):
        piece = ref[unit + k * tiles]
        turn = (k * reach - start) % LANES
        if turn:
            piece = pltpu.roll(piece, turn, 1)
        out = piece if k == 0 else jnp.where(lanes >= k * reach, piece, out)
    return out


def cell_copies(conc_hbm, temper_hbm, motion_hbm, base_ref, sem):
    copies = []
    for t in range(base_ref.shape[0]):
        start = 0
        for k, src in enumerate((conc_hbm, temper_hbm, motion_hbm)):
            dst = base_ref.at[t, pl.ds(start, src.shape[0])]
            part = src.at[:, pl.ds(t * LANES, LANES)]
            copies.append(pltpu.make_async_copy(part, dst, sem.at[3 * t + k]))
            start += src.shape[0]
    return copies


def mixture_kernel(
    conc_hbm, temper_hbm, motion_hbm, mass_hbm, size_hbm, energy_hbm, poly_hbm, base_hbm,
    slope_hbm, crit_hbm,
    state_ref, carried_ref, mat_ref, first_x, second_x, first_y, second_y, rate_ref,
    base_ref, mass_ref, size_ref, energy_ref, poly_ref, heat_ref, slope_ref, crit_ref, lin_ref, plane_ref,
    table_sem, cell_sem,
):
    tiles = base_ref.shape[0]
    width = temper_hbm.shape[0]
    species = mass_ref.shape[1]
    units = tiles * width
    cells = species * width
    pairs = (
        (mass_hbm, mass_ref), (size_hbm, size_ref), (energy_hbm, energy_ref),
        (poly_hbm, poly_ref), (base_hbm, heat_ref), (slope_hbm, slope_ref), (crit_hbm, crit_ref),
    )
    tables = [
        pltpu.make_async_copy(src, dst, table_sem.at[k]) for k, (src, dst) in enumerate(pairs)
    ]
    copies = cell_copies(conc_hbm, temper_hbm, motion_hbm, base_ref, cell_sem)
    for c in tables + copies:
        c.start()
    for c in tables:
        c.wait()
    write_matrix(
        mass_ref, size_ref, energy_ref, poly_ref, heat_ref, slope_ref, crit_ref, mat_ref
    )
    for c in copies:
        c.wait()
    ids = row_ids()

    batch = 2 if width % 2 == 0 else 1

    def place(j, i):
        return j * batch + i // tiles, i % tiles

    def read(j, i):
        x, t = place(j, i)
        mass = base_ref[t, pl.ds(x, species, stride=width), :]
        return mass, base_ref[t, pl.ds(cells + x, 1), :]

    def extra(j, i, u, temper, density):
        x, t = place(j, i)
        block = jnp.where(ids == 0, temper, jnp.where(ids == 4, density, 0.0))
        for c in range(3):
            row = base_ref[t, pl.ds(cells + (c + 1) * width + x, 1), :]
            block = jnp.where(ids == c + 1, row, block)
        state_ref[u, species : species + EXTRA, :] = block

    mix_products(units, batch * tiles, read, mat_ref, lin_ref, carried_ref, extra)
    rates = mix_cells(units, lin_ref, plane_ref)

    def step(x, best):
        for t in range(tiles):
            u = x * tiles + t
            front = plane_ref[0, pl.ds(u, 1), :]
            inv_density = plane_ref[1, pl.ds(u, 1), :]
            fraction = base_ref[t, pl.ds(x, species, stride=width), :] * inv_density
            share = (1.0 - fraction) / carried_ref[u, 0:species, :]
            state_ref[u, 0:species, :] = fraction
            carried_ref[u, 0:species, :] = front * share
            carried_ref[u, species : species + EXTRA, :] = coefficient_rows(plane_ref, u)
            state_ref[u, species + 5 : species + 6, :] = plane_ref[4, pl.ds(u, 1), :]
            state_ref[u, species + 6 : species + 7, :] = inv_density
            best = jnp.maximum(best, fold_rows(share, jnp.maximum) * (front * inv_density))
        return best

    best = lax.fori_loop(0, width, step, jnp.zeros((8, LANES), F32))
    top = jnp.maximum(jnp.max(best), jnp.max(rates))
    rate_ref[...] = jnp.full(rate_ref.shape, top, F32)

    even_x = lax.rem(lax.axis_index("gx"), 2) == 0
    upper = (width - 2) * tiles
    start_a = jnp.where(even_x, upper, 0)
    start_b = upper - start_a
    for k in range(2 * tiles):
        first_x[k] = state_ref[start_a + k]
        second_x[k] = state_ref[start_b + k]
    even_y = lax.rem(lax.axis_index("gy"), 2) == 0
    reach = 2 * LATERAL_ZONES
    per = LANES // reach
    for g in range(width // per):
        low = pack_cells(state_ref, g * per * tiles, tiles, 0, per)
        high = pack_cells(state_ref, g * per * tiles + tiles - 1, tiles, LANES - reach, per)
        first_y[g] = jnp.where(even_y, high, low)
        second_y[g] = jnp.where(even_y, low, high)


def weigh(before, here, after, beyond):
    value = 9.0 * (here + after) - (before + beyond)
    slope = 27.0 * (after - here) - (beyond - before)
    return value, slope


def only_value(before, here, after, beyond):
    return 9.0 * (here + after) - (before + beyond)


def z_shift(part, amount):
    zc = LATERAL_ZONES
    z_index = lax.broadcasted_iota(jnp.int32, part.shape, 1) % zc
    near = pltpu.roll(part, (LANES - amount) % LANES, 1)
    far = pltpu.roll(part, (zc - amount) if amount > 0 else LANES - (zc + amount), 1)
    if amount > 0:
        return jnp.where(z_index < zc - amount, near, far)
    return jnp.where(z_index >= -amount, near, far)


def face_weights(offset):
    value = np.select([offset == -1, offset == 0, offset == 1, offset == 2], [-1, 9, 9, -1], 0)
    slope = np.select([offset == -1, offset == 0, offset == 1, offset == 2], [1, -27, 27, -1], 0)
    return value, slope


def stencil_weights():
    zc = LATERAL_ZONES
    src, dst = np.meshgrid(np.arange(LANES), np.arange(LANES), indexing="ij")
    near = (src // zc) == (dst // zc)
    z_value, z_slope = face_weights(np.where(near, (src % zc - dst % zc + 1) % zc - 1, 9))

    def along_y(place):
        gap = place - dst
        return face_weights(np.where(gap % zc == 0, gap // zc, 9))

    y_value, y_slope = along_y(src)
    lent = along_y(np.where(src < 2 * zc, src + LANES, src - LANES))
    blocks = np.concatenate([z_value, y_value, z_slope, y_slope, *lent], axis=1)
    return np.concatenate([blocks, blocks], axis=0).astype(jnp.bfloat16)


def face_flux(f, h, species):
    value, slope = weigh(*f)
    product = only_value(*h) * slope
    drift = column_sum(product[:species]) * 0.0625
    return jnp.concatenate(
        [product[:species] - value[:species] * drift, product[species:]], axis=0
    )


def drifted(product, value, species):
    drift = column_sum(product[:species]) * 0.0625
    return jnp.concatenate([product[:species] - value[:species] * drift, product[species:]], axis=0)


def inner_kernel(
    batch, tiles, state_ref, carried_ref, weight_hbm, mat_ref, rate_ref, mat_out, weight_ref, sem
):
    units, rows, _ = state_ref.shape
    species = rows - EXTRA
    width = units // tiles
    zc = LATERAL_ZONES
    reach = 2 * zc
    wide = lax.broadcasted_iota(jnp.int32, (rows, LANES), 1)
    copy = pltpu.make_async_copy(weight_hbm, weight_ref, sem)
    copy.start()
    mat_out[...] = mat_ref[...]

    def along(t, carry):
        before = None
        for face in range(2, width - 1):
            f = [state_ref[(face + k) * tiles + t] for k in (-2, -1, 0, 1)]
            h = [carried_ref[(face + k) * tiles + t] for k in (-2, -1, 0, 1)]
            flux = face_flux(f, h, species)
            u = (face - 1) * tiles + t
            rate_ref[u] = flux if before is None else flux - before
            before = flux
        u = (width - 2) * tiles + t
        rate_ref[u] = -before
        for x in (0, width - 1):
            rate_ref[x * tiles + t] = jnp.zeros((rows, LANES), F32)
        return carry

    lax.fori_loop(0, tiles, along, 0)
    copy.wait()

    def wings(ref, j):
        own, lent = [], []
        for b in range(batch):
            f = [ref[(j * batch + b) * tiles + t] for t in range(tiles)]
            own += f
            for t in range(tiles):
                lent.append(jnp.where(wide < reach, f[(t + 1) % tiles], f[t - 1]))
        return [jnp.concatenate(split(jnp.concatenate(p, axis=0)), axis=1) for p in (own, lent)]

    def dot(a, start, stop):
        return jnp.dot(a, weight_ref[:, start * LANES : stop * LANES], preferred_element_type=F32)

    def work(j, carry):
        own, lent = wings(state_ref, j)
        first = dot(own, 0, 4)
        second = dot(lent, 4, 6)
        own, lent = wings(carried_ref, j)
        third = dot(own, 0, 2)
        fourth = dot(lent, 4, 5)
        for b in range(batch):
            fluxes = []
            for t in range(tiles):
                u = (j * batch + b) * tiles + t
                i = b * tiles + t
                rs = slice(i * rows, (i + 1) * rows)
                part = lambda m, k: m[rs, k * LANES : (k + 1) * LANES]
                flux = drifted(part(third, 0) * part(first, 2), part(first, 0), species)
                rate_ref[u] = rate_ref[u] + (flux - z_shift(flux, -1))
                value = part(first, 1) + part(second, 0)
                slope = part(first, 3) + part(second, 1)
                flux = drifted((part(third, 1) + part(fourth, 0)) * slope, value, species)
                if t == 0:
                    flux = jnp.where(wide >= zc, flux, 0.0)
                if t == tiles - 1:
                    flux = jnp.where(wide < LANES - reach, flux, 0.0)
                fluxes.append(flux)
            turned = [pltpu.roll(flux, zc, 1) for flux in fluxes]
            for t in range(tiles):
                u = (j * batch + b) * tiles + t
                back = jnp.where(wide >= zc, turned[t], turned[t - 1] if t > 0 else 0.0)
                rate_ref[u] = rate_ref[u] + (fluxes[t] - back)
        return carry

    lax.fori_loop(0, width // batch, work, 0)


def rim_kernel(
    state_ref, carried_ref, mat_ref, first_y, second_y, first_x, second_x, partial_ref,
    rate_ref,
    halo_ref, halo_carried, lin_ref, plane_ref, edge_ref, pack_ref, halo_sem,
):
    units, rows, _ = state_ref.shape
    species = rows - EXTRA
    packs = first_y.shape[0]
    half = first_x.shape[0]
    tiles = half // 2
    width = units // tiles
    zc = LATERAL_ZONES
    reach = 2 * zc
    per = LANES // reach
    me, peers = lax.axis_index("gx"), lax.axis_size("gx")
    even_x = lax.rem(me, 2) == 0
    even_y = lax.rem(lax.axis_index("gy"), 2) == 0
    at_start, at_end = me == 0, me == peers - 1
    skip = 2 * packs
    low_x, low_y = jnp.where(even_x, half, 0), jnp.where(even_y, packs, 0)
    halos = [
        pltpu.make_async_copy(src, halo_ref.at[pl.ds(start, src.shape[0])], halo_sem.at[k])
        for k, (src, start) in enumerate(
            (
                (first_y, low_y),
                (second_y, packs - low_y),
                (first_x, skip + low_x),
                (second_x, skip + half - low_x),
            )
        )
    ]
    for c in halos:
        c.start()
    for g in range(packs):
        unit = g * per * tiles
        last = unit + tiles - 1
        for k, ref in enumerate((state_ref, carried_ref)):
            for i, (at, start) in enumerate(
                ((unit, 0), (unit, reach), (last, LANES - 2 * reach), (last, LANES - reach))
            ):
                pack_ref[(4 * k + i) * packs + g] = pack_cells(ref, at, tiles, start, per)

    for c in halos:
        c.wait()

    @pl.when(at_start)
    def _():
        for k in range(half):
            halo_ref[skip + k] = state_ref[k % tiles]

    @pl.when(at_end)
    def _():
        for k in range(half):
            halo_ref[skip + half + k] = state_ref[units - tiles + k % tiles]

    total = skip + 2 * half
    group = next(n for n in (8, 6, 4, 3, 2, 1) if total % n == 0)
    mix_halo(total, group, halo_ref, mat_ref, lin_ref, plane_ref, halo_carried)

    ids = row_ids()
    wide = lax.broadcasted_iota(jnp.int32, (rows, LANES), 1)
    lower = wide % reach < zc

    def between(p, q):
        return jnp.where(lower, pltpu.roll(p, LANES - zc, 1), pltpu.roll(q, zc, 1))

    for g in range(packs):
        stencils = []
        for i, halo in enumerate((halo_ref, halo_carried)):
            below, above = halo[g], halo[packs + g]
            low, up, down, high = [pack_ref[(4 * i + k) * packs + g] for k in range(4)]
            stencils.append(
                (
                    (below, between(below, low), low, between(low, up)),
                    (between(down, high), high, between(high, above), above),
                )
            )
        flux = face_flux(stencils[0][0], stencils[1][0], species)
        edge_ref[g] = jnp.where(lower, pltpu.roll(flux, LANES - zc, 1), 0.0) - flux
        flux = face_flux(stencils[0][1], stencils[1][1], species)
        edge_ref[packs + g] = flux - jnp.where(lower, 0.0, pltpu.roll(flux, zc, 1))

    for t in range(tiles):

        def row(inner, outer, x):
            if x < 0:
                return outer[skip + (x + 2) * tiles + t]
            if x >= width:
                return outer[skip + half + (x - width) * tiles + t]
            return inner[x * tiles + t]

        flux = {}
        for face in (0, 1, width - 1, width):
            f = [row(state_ref, halo_ref, face + k) for k in (-2, -1, 0, 1)]
            h = [row(carried_ref, halo_carried, face + k) for k in (-2, -1, 0, 1)]
            flux[face] = face_flux(f, h, species)
        for x in range(width):
            u = x * tiles + t
            g, k = divmod(x, per)
            total = partial_ref[u]
            if x + 1 in flux:
                total = total + flux[x + 1]
            if x in flux:
                total = total - flux[x]
            if t == 0:
                edge = edge_ref[g]
                edge = pltpu.roll(edge, LANES - k * reach, 1) if k else edge
                total = total + jnp.where(wide < reach, edge, 0.0)
            if t == tiles - 1:
                edge = edge_ref[packs + g]
                turn = (LANES - (k + 1) * reach) % LANES
                edge = pltpu.roll(edge, turn, 1) if turn else edge
                total = total + jnp.where(wide >= LANES - reach, edge, 0.0)
            inv_heat = state_ref[u, species + 5 : species + 6, :]
            inv_density = state_ref[u, species + 6 : species + 7, :]
            scale = jnp.where(ids == 0, inv_heat, inv_density)
            total = jnp.concatenate([total[:species], total[species:] * scale], axis=0)
            rate_ref[u] = total


def finish_kernel(
    state_ref, rate_ref, top_ref,
    conc_next, temper_next, motion_next, interval_next,
    next_ref, interval_ref, sem,
):
    tiles, _, _ = next_ref.shape
    units, rows, _ = state_ref.shape
    species = rows - EXTRA
    width = units // tiles
    interval = CFL_NUMBER / jnp.max(top_ref[...], axis=(0, 1), keepdims=True)
    interval_ref[...] = interval
    factor = interval * (1.0 / 384.0)
    outs = [pltpu.make_async_copy(interval_ref, interval_next, sem.at[3 * tiles])]
    outs[0].start()
    for t in range(tiles):
        for x in range(width):
            u = x * tiles + t
            density = state_ref[u, species + 4 : species + 5, :]
            here = jnp.concatenate(
                [state_ref[u, 0:species, :] * density, state_ref[u, species:, :]], axis=0
            )
            next_ref[t, pl.ds(x, rows, stride=width), :] = here + factor * rate_ref[u]
        start = 0
        for k, dst in enumerate((conc_next, temper_next, motion_next)):
            src = next_ref.at[t, pl.ds(start, dst.shape[0])]
            part = dst.at[:, pl.ds(t * LANES, LANES)]
            outs.append(pltpu.make_async_copy(src, part, sem.at[3 * t + k]))
            outs[-1].start()
            start += dst.shape[0]
    for c in outs:
        c.wait()


def call(kernel, outs, ins, scratch=()):
    shapes, specs = [], []
    for shape, dtype, place in outs:
        space = {True: pltpu.VMEM, pl.ANY: pltpu.HBM}.get(place, jax.ShapeDtypeStruct)
        shapes.append(space(shape, dtype))
        specs.append(pl.BlockSpec(memory_space=pl.ANY if place is pl.ANY else VMEM))
    run = pl.pallas_call(
        kernel,
        out_shape=shapes,
        in_specs=[
            pl.BlockSpec(memory_space={True: VMEM, pl.ANY: pltpu.HBM, None: pl.ANY}[m]) for m in ins
        ],
        out_specs=specs,
        scratch_shapes=list(scratch),
        compiler_params=pltpu.CompilerParams(vmem_limit_bytes=16 << 20),
    )

    def apply(*args):
        return run(
            *[
                a
                if m is None
                else pltpu.with_memory_space_constraint(a, pltpu.VMEM if m is True else pltpu.HBM)
                for a, m in zip(args, ins)
            ]
        )

    return apply


def body(
    component_concentration,
    thermal_level,
    motion_vector,
    component_weight_per_mole,
    collision_size_third,
    potential_depth_volume,
    binary_drag_logpoly,
    specific_warmth_intercept,
    specific_warmth_gradient,
    component_threshold_stress,
):
    species, width, line = component_concentration.shape
    terms = binary_drag_logpoly.shape[0]
    tiles = line // LANES
    units = width * tiles
    rows = species + EXTRA
    per = LANES // (2 * LATERAL_ZONES)
    packs = width // per
    nx, ny = lax.axis_size("gx"), lax.axis_size("gy")
    devices = nx * ny
    conc = component_concentration.reshape(species * width, line)
    motion = motion_vector.reshape(3 * width, line)
    mat_rows = (terms + 2) * species + 16
    count = (species + 4) * width
    keep = True
    field = ((units, rows, LANES), F32, keep)
    mix_scratch = lambda n: [pltpu.VMEM((n * 8, LANES), F32), pltpu.VMEM((5, n, LANES), F32)]
    state, carried, mat, first_x, second_x, first_y, second_y, rate = call(
        mixture_kernel,
        [
            field,
            field,
            ((mat_rows, 2 * species), jnp.bfloat16, keep),
            ((2 * tiles, rows, LANES), F32, keep),
            ((2 * tiles, rows, LANES), F32, keep),
            ((packs, rows, LANES), F32, keep),
            ((packs, rows, LANES), F32, keep),
            ((devices, LANES), F32, keep),
        ],
        [pl.ANY] * 10,
        [
            pltpu.VMEM((tiles, count, LANES), F32),
            pltpu.VMEM((1, species), F32),
            pltpu.VMEM((species, species), F32),
            pltpu.VMEM((species, species), F32),
            pltpu.VMEM((terms * species, species), F32),
            pltpu.VMEM((1, species), F32),
            pltpu.VMEM((1, species), F32),
            pltpu.VMEM((1, species), F32),
        ]
        + mix_scratch(units)
        + [pltpu.SemaphoreType.DMA((n,)) for n in (7, 3 * tiles)],
    )(
        conc,
        thermal_level,
        motion,
        component_weight_per_mole[None],
        collision_size_third,
        potential_depth_volume,
        binary_drag_logpoly.reshape(terms * species, species),
        specific_warmth_intercept[None],
        specific_warmth_gradient[None],
        component_threshold_stress[None],
    )
    top = lax.all_to_all(rate, ("gx", "gy"), 0, 0, tiled=True)
    pair_first = lambda n: [(i, i ^ 1) for i in range(n)]
    pair_second = lambda n: [(i, (i + 1) % n if i % 2 else (i - 1) % n) for i in range(n)]
    inside = [(i, j) for i, j in pair_second(nx) if abs(i - j) == 1]
    got_first_x = lax.ppermute(first_x, "gx", pair_first(nx))
    got_second_x = lax.ppermute(second_x, "gx", inside)
    got_first_y = lax.ppermute(first_y, "gy", pair_first(ny))
    got_second_y = lax.ppermute(second_y, "gy", pair_second(ny))
    batch = 2 if width % 2 == 0 else 1
    weights = jnp.asarray(stencil_weights())
    inner, mat = call(
        functools.partial(inner_kernel, batch, tiles),
        [
            field,
            ((mat_rows, 2 * species), jnp.bfloat16, keep),
        ],
        [keep, keep, pl.ANY, keep],
        [pltpu.VMEM(weights.shape, weights.dtype), pltpu.SemaphoreType.DMA(())],
    )(state, carried, weights, mat)
    halos = 2 * packs + 4 * tiles
    (total,) = call(
        rim_kernel,
        [field],
        [keep] * 3 + [None] * 4 + [keep],
        [
            pltpu.VMEM((halos, rows, LANES), F32),
            pltpu.VMEM((halos, rows, LANES), F32),
        ]
        + mix_scratch(halos)
        + [
            pltpu.VMEM((2 * packs, rows, LANES), F32),
            pltpu.VMEM((8 * packs, rows, LANES), F32),
            pltpu.SemaphoreType.DMA((4,)),
        ],
    )(
        state,
        carried,
        mat,
        got_first_y,
        got_second_y,
        got_first_x,
        got_second_x,
        inner,
    )
    conc_next, temper_next, motion_next, interval = call(
        finish_kernel,
        [
            (conc.shape, F32, pl.ANY),
            (thermal_level.shape, F32, pl.ANY),
            (motion.shape, F32, pl.ANY),
            ((1, 1), F32, pl.ANY),
        ],
        [keep] * 3,
        [
            pltpu.VMEM((tiles, rows * width, LANES), F32),
            pltpu.VMEM((1, 1), F32),
            pltpu.SemaphoreType.DMA((3 * tiles + 1,)),
        ],
    )(state, total, top)
    return (
        conc_next.reshape(component_concentration.shape),
        motion_next.reshape(motion_vector.shape),
        temper_next,
        interval.reshape(()),
    )


def solution(mesh):
    in_specs = (
        P(None, "gx", "gy"),
        P("gx", "gy"),
        P(None, "gx", "gy"),
    ) + (P(),) * 7
    out_specs = (P(None, "gx", "gy"), P(None, "gx", "gy"), P("gx", "gy"), P())
    return jax.shard_map(body, mesh=mesh, in_specs=in_specs, out_specs=out_specs, check_vma=False)
```

```python
import functools

import jax
import jax.numpy as jnp
import numpy as np
from jax import lax
from jax.experimental import pallas as pl
from jax.experimental.pallas import tpu as pltpu
from jax.sharding import PartitionSpec as P


LATERAL_ZONES = 16
CFL_NUMBER = 0.12
GAS_SCALE = 0.01
BETA = 0.7862
LANES = 128
EXTRA = 8
F32 = jnp.float32
VMEM = pltpu.MemorySpace.VMEM


def row_ids():
    return lax.broadcasted_iota(jnp.int32, (EXTRA, LANES), 0)


def split(value):
    high = value.astype(jnp.bfloat16)
    low = (value - high.astype(F32)).astype(jnp.bfloat16)
    return high, low


def fold_rows(value, op):
    parts = [value[8 * i : 8 * i + 8] for i in range(value.shape[0] // 8)]
    while len(parts) > 1:
        half = [op(parts[i], parts[i + 1]) for i in range(0, len(parts) - 1, 2)]
        parts = half + ([parts[-1]] if len(parts) % 2 else [])
    return parts[0]


def column_sum(value):
    return jnp.sum(fold_rows(value, jnp.add), axis=0, keepdims=True)


def write_matrix(mass_ref, size_ref, energy_ref, poly_ref, base_ref, slope_ref, crit_ref, mat_ref):
    species = mass_ref.shape[1]
    terms = poly_ref.shape[0] // species
    inverse = 1.0 / mass_ref[...]
    rows = lax.broadcasted_iota(jnp.int32, (species, species), 0)
    cols = lax.broadcasted_iota(jnp.int32, (species, species), 1)
    same = rows == cols
    column = jnp.sum(
        jnp.where(same, jnp.broadcast_to(inverse, (species, species)), 0.0), axis=1, keepdims=True
    )

    def put(start, block):
        high, low = split(block)
        high, low = high.astype(F32), low.astype(F32)
        mat_ref[start : start + block.shape[0], :] = jnp.concatenate(
            [high, low], axis=1
        ).astype(jnp.bfloat16)

    for k in range(terms):
        block = jnp.where(same, 0.0, poly_ref[k * species : (k + 1) * species, :])
        put(k * species, block * inverse)
    put(terms * species, size_ref[...] * inverse * column)
    put((terms + 1) * species, energy_ref[...] * inverse * column)
    lin = lax.broadcasted_iota(jnp.int32, (16, species), 0)
    block = jnp.where(lin == 0, 1.0, 0.0)
    for k, row in enumerate(
        (inverse, base_ref[...] * inverse, slope_ref[...] * inverse, crit_ref[...] * inverse)
    ):
        block = jnp.where(lin == k + 1, row, block)
    put((terms + 2) * species, block)


def mix_products(units, group, read, mat_ref, lin_ref, resist_ref, extra=None, unit=None, ready=None):
    ids = row_ids()

    def step(j, carry):
        pieces = [read(j, i) for i in range(group)]
        mass = [p[0] for p in pieces]
        species = mass[0].shape[0]
        terms = mat_ref.shape[0] // species - 2
        wide = jnp.concatenate(mass, axis=1)
        high, low = split(wide)
        stacked = jnp.concatenate([high, high, low, low], axis=0)
        both = jnp.concatenate([mat_ref[...], mat_ref[...]], axis=1)
        product = jnp.dot(both, stacked, preferred_element_type=F32)
        for i, (m, temper) in enumerate(pieces):
            part = product[:, i * LANES : (i + 1) * LANES]
            u = j * group + i if unit is None else unit(j, i)
            logt = jnp.log(temper)
            total = part[(terms - 1) * species : terms * species]
            for k in range(terms - 2, -1, -1):
                total = total * logt + part[k * species : (k + 1) * species]
            resist_ref[u, 0:species, :] = total
            size = column_sum(m * part[terms * species : (terms + 1) * species])
            energy = column_sum(m * part[(terms + 1) * species : (terms + 2) * species])
            lin = part[(terms + 2) * species : (terms + 2) * species + 8]
            lin = jnp.where(ids == 5, size, jnp.where(ids == 6, energy, lin))
            lin = jnp.where(ids == 7, temper, lin)
            row = u * 8 if isinstance(u, int) else pl.multiple_of(u * 8, 8)
            lin_ref[pl.ds(row, 8), :] = lin
            if extra is not None:
                extra(j, i, u, temper, part[(terms + 2) * species : (terms + 2) * species + 1])
        return carry

    if ready is None:
        lax.fori_loop(0, units // group, step, 0)
    else:
        for j in range(units // group):
            ready(j)
            step(j, 0)


def mix_cells(units, lin_ref, plane_ref):
    def plane(k):
        return lin_ref[pl.ds(k, units, stride=8), :]

    density, moles, base, slope, crit, size, energy, temper = [plane(k) for k in range(8)]
    reduced = temper * size / energy
    collision = (
        1.16145 * jnp.exp(-0.14874 * jnp.log(reduced))
        + 0.52487 * jnp.exp(-0.7732 * reduced)
        + 2.16178 * jnp.exp(-2.43787 * reduced)
    )
    inv_moles = 1.0 / moles
    mean_mass = density * inv_moles
    size_mix = size * inv_moles * inv_moles
    viscosity = (
        (40.785 * (0.809 * 0.809))
        * jnp.sqrt(mean_mass * temper)
        / (jnp.exp((2.0 / 3.0) * jnp.log(size_mix)) * collision)
    )
    heat_total = base + slope * temper
    excess = heat_total * inv_moles - 2.5
    ratio = reduced * (1.0 / 1.2593)
    zeta = 2.0 + 10.5 * ratio * ratio
    psi = 1.0 + excess * (0.215 + 0.28288 * excess - 1.061 * BETA + 0.26665 * zeta) / (
        0.6366 + BETA * zeta + (1.061 * BETA) * excess
    )
    conduct = 7.452 * viscosity * psi / mean_mass
    over = GAS_SCALE * temper * moles * moles / crit
    takahashi = 1.0 / (1.0 + 0.25 * over * over)
    front = density * takahashi * jnp.sqrt(temper) * (1.0 / GAS_SCALE)
    inv_density = 1.0 / density
    inv_heat = 1.0 / heat_total
    plane_ref[0] = front
    plane_ref[1] = inv_density
    plane_ref[2] = viscosity
    plane_ref[3] = conduct
    plane_ref[4] = inv_heat
    return jnp.maximum(viscosity * inv_density, conduct * inv_heat)


def coefficient_rows(plane_ref, u):
    ids = row_ids()
    visc = plane_ref[2, pl.ds(u, 1), :]
    cond = plane_ref[3, pl.ds(u, 1), :]
    return jnp.where(ids == 0, cond, jnp.where(ids < 4, visc, 0.0))


def mix_halo(units, group, state_ref, mat_ref, lin_ref, plane_ref, carried_ref):
    species = state_ref.shape[1] - EXTRA

    def read(j, i):
        u = j * group + i
        density = state_ref[u, species + 4 : species + 5, :]
        return state_ref[u, 0:species, :] * density, state_ref[u, species : species + 1, :]

    mix_products(units, group, read, mat_ref, lin_ref, carried_ref)
    mix_cells(units, lin_ref, plane_ref)

    def step(u, carry):
        front = plane_ref[0, pl.ds(u, 1), :]
        fraction = state_ref[u, 0:species, :]
        carried_ref[u, 0:species, :] = front * ((1.0 - fraction) / carried_ref[u, 0:species, :])
        carried_ref[u, species : species + EXTRA, :] = coefficient_rows(plane_ref, u)
        return carry

    lax.fori_loop(0, units, step, 0)


def pack_cells(ref, unit, tiles, start, per):
    reach = LANES // per
    rows = ref.shape[1]
    lanes = lax.broadcasted_iota(jnp.int32, (rows, LANES), 1)
    out = None
    for k in range(per):
        piece = ref[unit + k * tiles]
        turn = (k * reach - start) % LANES
        if turn:
            piece = pltpu.roll(piece, turn, 1)
        out = piece if k == 0 else jnp.where(lanes >= k * reach, piece, out)
    return out


def cell_copies(conc_hbm, temper_hbm, motion_hbm, base_ref, sem):
    copies = []
    for t in range(base_ref.shape[0]):
        start = 0
        for k, src in enumerate((conc_hbm, temper_hbm, motion_hbm)):
            dst = base_ref.at[t, pl.ds(start, src.shape[0])]
            part = src.at[:, pl.ds(t * LANES, LANES)]
            copies.append(pltpu.make_async_copy(part, dst, sem.at[3 * t + k]))
            start += src.shape[0]
    return copies


def mixture_kernel(
    conc_hbm, temper_hbm, motion_hbm, mass_hbm, size_hbm, energy_hbm, poly_hbm, base_hbm,
    slope_hbm, crit_hbm,
    state_ref, carried_ref, mat_ref, first_x, second_x, first_y, second_y, rate_hbm,
    rate_ref, base_ref, mass_ref, size_ref, energy_ref, poly_ref, heat_ref, slope_ref, crit_ref, lin_ref, plane_ref,
    table_sem, cell_sem, rate_sem,
):
    tiles = base_ref.shape[0]
    width = temper_hbm.shape[0]
    species = mass_ref.shape[1]
    units = tiles * width
    cells = species * width
    pairs = (
        (mass_hbm, mass_ref), (size_hbm, size_ref), (energy_hbm, energy_ref),
        (poly_hbm, poly_ref), (base_hbm, heat_ref), (slope_hbm, slope_ref), (crit_hbm, crit_ref),
    )
    tables = [
        pltpu.make_async_copy(src, dst, table_sem.at[k]) for k, (src, dst) in enumerate(pairs)
    ]
    copies = cell_copies(conc_hbm, temper_hbm, motion_hbm, base_ref, cell_sem)
    for c in tables + copies:
        c.start()
    for c in tables:
        c.wait()
    write_matrix(
        mass_ref, size_ref, energy_ref, poly_ref, heat_ref, slope_ref, crit_ref, mat_ref
    )
    ids = row_ids()

    def ready(t):
        for c in copies if t == 0 else ():
            c.wait()

    def read(t, x):
        mass = base_ref[t, pl.ds(x, species, stride=width), :]
        return mass, base_ref[t, pl.ds(cells + x, 1), :]

    def extra(t, x, u, temper, density):
        block = jnp.where(ids == 0, temper, jnp.where(ids == 4, density, 0.0))
        for c in range(3):
            row = base_ref[t, pl.ds(cells + (c + 1) * width + x, 1), :]
            block = jnp.where(ids == c + 1, row, block)
        state_ref[u, species : species + EXTRA, :] = block

    unit = lambda t, x: x * tiles + t
    mix_products(units, width, read, mat_ref, lin_ref, carried_ref, extra, unit, ready)
    rates = mix_cells(units, lin_ref, plane_ref)

    def step(x, best):
        for t in range(tiles):
            u = x * tiles + t
            front = plane_ref[0, pl.ds(u, 1), :]
            inv_density = plane_ref[1, pl.ds(u, 1), :]
            fraction = base_ref[t, pl.ds(x, species, stride=width), :] * inv_density
            share = (1.0 - fraction) / carried_ref[u, 0:species, :]
            state_ref[u, 0:species, :] = fraction
            carried_ref[u, 0:species, :] = front * share
            carried_ref[u, species : species + EXTRA, :] = coefficient_rows(plane_ref, u)
            state_ref[u, species + 5 : species + 6, :] = plane_ref[4, pl.ds(u, 1), :]
            state_ref[u, species + 6 : species + 7, :] = inv_density
            best = jnp.maximum(best, fold_rows(share, jnp.maximum) * (front * inv_density))
        return best

    best = jnp.zeros((8, LANES), F32)
    for x in range(width):
        best = step(x, best)
    top = jnp.maximum(jnp.max(best), jnp.max(rates))
    rate_ref[...] = jnp.full(rate_ref.shape, top, F32)
    send = pltpu.make_async_copy(rate_ref, rate_hbm, rate_sem)
    send.start()

    even_x = lax.rem(lax.axis_index("gx"), 2) == 0
    upper = (width - 2) * tiles
    start_a = jnp.where(even_x, upper, 0)
    start_b = upper - start_a
    for k in range(2 * tiles):
        first_x[k] = state_ref[start_a + k]
        second_x[k] = state_ref[start_b + k]
    even_y = lax.rem(lax.axis_index("gy"), 2) == 0
    reach = 2 * LATERAL_ZONES
    per = LANES // reach
    for g in range(width // per):
        low = pack_cells(state_ref, g * per * tiles, tiles, 0, per)
        high = pack_cells(state_ref, g * per * tiles + tiles - 1, tiles, LANES - reach, per)
        first_y[g] = jnp.where(even_y, high, low)
        second_y[g] = jnp.where(even_y, low, high)
    send.wait()


def weigh(before, here, after, beyond):
    value = 9.0 * (here + after) - (before + beyond)
    slope = 27.0 * (after - here) - (beyond - before)
    return value, slope


def only_value(before, here, after, beyond):
    return 9.0 * (here + after) - (before + beyond)


def z_shift(part, amount):
    zc = LATERAL_ZONES
    z_index = lax.broadcasted_iota(jnp.int32, part.shape, 1) % zc
    near = pltpu.roll(part, (LANES - amount) % LANES, 1)
    far = pltpu.roll(part, (zc - amount) if amount > 0 else LANES - (zc + amount), 1)
    if amount > 0:
        return jnp.where(z_index < zc - amount, near, far)
    return jnp.where(z_index >= -amount, near, far)


def face_weights(offset):
    value = np.select([offset == -1, offset == 0, offset == 1, offset == 2], [-1, 9, 9, -1], 0)
    slope = np.select([offset == -1, offset == 0, offset == 1, offset == 2], [1, -27, 27, -1], 0)
    return value, slope


def stencil_weights():
    zc = LATERAL_ZONES
    src, dst = np.meshgrid(np.arange(LANES), np.arange(LANES), indexing="ij")
    near = (src // zc) == (dst // zc)
    z_value, z_slope = face_weights(np.where(near, (src % zc - dst % zc + 1) % zc - 1, 9))

    def along_y(place):
        gap = place - dst
        return face_weights(np.where(gap % zc == 0, gap // zc, 9))

    y_value, y_slope = along_y(src)
    lent = along_y(np.where(src < 2 * zc, src + LANES, src - LANES))
    blocks = np.concatenate([z_value, y_value, z_slope, y_slope, *lent], axis=1)
    return np.concatenate([blocks, blocks], axis=0).astype(jnp.bfloat16)


def face_flux(f, h, species):
    value, slope = weigh(*f)
    product = only_value(*h) * slope
    drift = column_sum(product[:species]) * 0.0625
    return jnp.concatenate(
        [product[:species] - value[:species] * drift, product[species:]], axis=0
    )


def drifted(product, value, species):
    drift = column_sum(product[:species]) * 0.0625
    return jnp.concatenate([product[:species] - value[:species] * drift, product[species:]], axis=0)


def inner_kernel(
    batch, tiles, state_ref, carried_ref, weight_hbm, mat_ref, rate_ref, mat_out, weight_ref, sem
):
    units, rows, _ = state_ref.shape
    species = rows - EXTRA
    width = units // tiles
    zc = LATERAL_ZONES
    reach = 2 * zc
    wide = lax.broadcasted_iota(jnp.int32, (rows, LANES), 1)
    copy = pltpu.make_async_copy(weight_hbm, weight_ref, sem)
    copy.start()
    mat_out[...] = mat_ref[...]

    def along(t, carry):
        before = None
        for face in range(2, width - 1):
            f = [state_ref[(face + k) * tiles + t] for k in (-2, -1, 0, 1)]
            h = [carried_ref[(face + k) * tiles + t] for k in (-2, -1, 0, 1)]
            flux = face_flux(f, h, species)
            u = (face - 1) * tiles + t
            rate_ref[u] = flux if before is None else flux - before
            before = flux
        u = (width - 2) * tiles + t
        rate_ref[u] = -before
        for x in (0, width - 1):
            rate_ref[x * tiles + t] = jnp.zeros((rows, LANES), F32)
        return carry

    lax.fori_loop(0, tiles, along, 0)
    copy.wait()

    def wings(ref, j):
        own, lent = [], []
        for b in range(batch):
            f = [ref[(j * batch + b) * tiles + t] for t in range(tiles)]
            own += f
            for t in range(tiles):
                lent.append(jnp.where(wide < reach, f[(t + 1) % tiles], f[t - 1]))
        return [jnp.concatenate(split(jnp.concatenate(p, axis=0)), axis=1) for p in (own, lent)]

    def dot(a, start, stop):
        return jnp.dot(a, weight_ref[:, start * LANES : stop * LANES], preferred_element_type=F32)

    def work(j, carry):
        own, lent = wings(state_ref, j)
        first = dot(own, 0, 4)
        second = dot(lent, 4, 6)
        own, lent = wings(carried_ref, j)
        third = dot(own, 0, 2)
        fourth = dot(lent, 4, 5)
        for b in range(batch):
            fluxes = []
            for t in range(tiles):
                u = (j * batch + b) * tiles + t
                i = b * tiles + t
                rs = slice(i * rows, (i + 1) * rows)
                part = lambda m, k: m[rs, k * LANES : (k + 1) * LANES]
                flux = drifted(part(third, 0) * part(first, 2), part(first, 0), species)
                rate_ref[u] = rate_ref[u] + (flux - z_shift(flux, -1))
                value = part(first, 1) + part(second, 0)
                slope = part(first, 3) + part(second, 1)
                flux = drifted((part(third, 1) + part(fourth, 0)) * slope, value, species)
                if t == 0:
                    flux = jnp.where(wide >= zc, flux, 0.0)
                if t == tiles - 1:
                    flux = jnp.where(wide < LANES - reach, flux, 0.0)
                fluxes.append(flux)
            turned = [pltpu.roll(flux, zc, 1) for flux in fluxes]
            for t in range(tiles):
                u = (j * batch + b) * tiles + t
                back = jnp.where(wide >= zc, turned[t], turned[t - 1] if t > 0 else 0.0)
                rate_ref[u] = rate_ref[u] + (fluxes[t] - back)
        return carry

    lax.fori_loop(0, width // batch, work, 0)


def rim_kernel(
    state_ref, carried_ref, mat_ref, first_y, second_y, first_x, second_x, partial_ref,
    rate_ref,
    halo_ref, halo_carried, lin_ref, plane_ref, edge_ref, pack_ref, halo_sem,
):
    units, rows, _ = state_ref.shape
    species = rows - EXTRA
    packs = first_y.shape[0]
    half = first_x.shape[0]
    tiles = half // 2
    width = units // tiles
    zc = LATERAL_ZONES
    reach = 2 * zc
    per = LANES // reach
    me, peers = lax.axis_index("gx"), lax.axis_size("gx")
    even_x = lax.rem(me, 2) == 0
    even_y = lax.rem(lax.axis_index("gy"), 2) == 0
    at_start, at_end = me == 0, me == peers - 1
    skip = 2 * packs
    low_x, low_y = jnp.where(even_x, half, 0), jnp.where(even_y, packs, 0)
    halos = [
        pltpu.make_async_copy(src, halo_ref.at[pl.ds(start, src.shape[0])], halo_sem.at[k])
        for k, (src, start) in enumerate(
            (
                (first_y, low_y),
                (second_y, packs - low_y),
                (first_x, skip + low_x),
                (second_x, skip + half - low_x),
            )
        )
    ]
    for c in halos:
        c.start()
    for g in range(packs):
        unit = g * per * tiles
        last = unit + tiles - 1
        for k, ref in enumerate((state_ref, carried_ref)):
            for i, (at, start) in enumerate(
                ((unit, 0), (unit, reach), (last, LANES - 2 * reach), (last, LANES - reach))
            ):
                pack_ref[(4 * k + i) * packs + g] = pack_cells(ref, at, tiles, start, per)

    for c in halos:
        c.wait()

    @pl.when(at_start)
    def _():
        for k in range(half):
            halo_ref[skip + k] = state_ref[k % tiles]

    @pl.when(at_end)
    def _():
        for k in range(half):
            halo_ref[skip + half + k] = state_ref[units - tiles + k % tiles]

    total = skip + 2 * half
    group = next(n for n in (8, 6, 4, 3, 2, 1) if total % n == 0)
    mix_halo(total, group, halo_ref, mat_ref, lin_ref, plane_ref, halo_carried)

    ids = row_ids()
    wide = lax.broadcasted_iota(jnp.int32, (rows, LANES), 1)
    lower = wide % reach < zc

    def between(p, q):
        return jnp.where(lower, pltpu.roll(p, LANES - zc, 1), pltpu.roll(q, zc, 1))

    for g in range(packs):
        stencils = []
        for i, halo in enumerate((halo_ref, halo_carried)):
            below, above = halo[g], halo[packs + g]
            low, up, down, high = [pack_ref[(4 * i + k) * packs + g] for k in range(4)]
            stencils.append(
                (
                    (below, between(below, low), low, between(low, up)),
                    (between(down, high), high, between(high, above), above),
                )
            )
        flux = face_flux(stencils[0][0], stencils[1][0], species)
        edge_ref[g] = jnp.where(lower, pltpu.roll(flux, LANES - zc, 1), 0.0) - flux
        flux = face_flux(stencils[0][1], stencils[1][1], species)
        edge_ref[packs + g] = flux - jnp.where(lower, 0.0, pltpu.roll(flux, zc, 1))

    for t in range(tiles):

        def row(inner, outer, x):
            if x < 0:
                return outer[skip + (x + 2) * tiles + t]
            if x >= width:
                return outer[skip + half + (x - width) * tiles + t]
            return inner[x * tiles + t]

        flux = {}
        for face in (0, 1, width - 1, width):
            f = [row(state_ref, halo_ref, face + k) for k in (-2, -1, 0, 1)]
            h = [row(carried_ref, halo_carried, face + k) for k in (-2, -1, 0, 1)]
            flux[face] = face_flux(f, h, species)
        for x in range(width):
            u = x * tiles + t
            g, k = divmod(x, per)
            total = partial_ref[u]
            if x + 1 in flux:
                total = total + flux[x + 1]
            if x in flux:
                total = total - flux[x]
            if t == 0:
                edge = edge_ref[g]
                edge = pltpu.roll(edge, LANES - k * reach, 1) if k else edge
                total = total + jnp.where(wide < reach, edge, 0.0)
            if t == tiles - 1:
                edge = edge_ref[packs + g]
                turn = (LANES - (k + 1) * reach) % LANES
                edge = pltpu.roll(edge, turn, 1) if turn else edge
                total = total + jnp.where(wide >= LANES - reach, edge, 0.0)
            inv_heat = state_ref[u, species + 5 : species + 6, :]
            inv_density = state_ref[u, species + 6 : species + 7, :]
            scale = jnp.where(ids == 0, inv_heat, inv_density)
            total = jnp.concatenate([total[:species], total[species:] * scale], axis=0)
            rate_ref[u] = total


def finish_kernel(
    state_ref, rate_ref, top_ref,
    conc_next, temper_next, motion_next, interval_next,
    next_ref, interval_ref, sem,
):
    tiles, _, _ = next_ref.shape
    units, rows, _ = state_ref.shape
    species = rows - EXTRA
    width = units // tiles
    interval = CFL_NUMBER / jnp.max(top_ref[...], axis=(0, 1), keepdims=True)
    interval_ref[...] = interval
    factor = interval * (1.0 / 384.0)
    outs = [pltpu.make_async_copy(interval_ref, interval_next, sem.at[3 * tiles])]
    outs[0].start()
    for t in range(tiles):
        for x in range(width):
            u = x * tiles + t
            density = state_ref[u, species + 4 : species + 5, :]
            here = jnp.concatenate(
                [state_ref[u, 0:species, :] * density, state_ref[u, species:, :]], axis=0
            )
            next_ref[t, pl.ds(x, rows, stride=width), :] = here + factor * rate_ref[u]
        start = 0
        for k, dst in enumerate((conc_next, temper_next, motion_next)):
            src = next_ref.at[t, pl.ds(start, dst.shape[0])]
            part = dst.at[:, pl.ds(t * LANES, LANES)]
            outs.append(pltpu.make_async_copy(src, part, sem.at[3 * t + k]))
            outs[-1].start()
            start += dst.shape[0]
    for c in outs:
        c.wait()


def call(kernel, outs, ins, scratch=()):
    shapes, specs = [], []
    for shape, dtype, place in outs:
        space = {True: pltpu.VMEM, pl.ANY: pltpu.HBM}.get(place, jax.ShapeDtypeStruct)
        shapes.append(space(shape, dtype))
        specs.append(pl.BlockSpec(memory_space=pl.ANY if place is pl.ANY else VMEM))
    run = pl.pallas_call(
        kernel,
        out_shape=shapes,
        in_specs=[
            pl.BlockSpec(memory_space={True: VMEM, pl.ANY: pltpu.HBM, None: pl.ANY}[m]) for m in ins
        ],
        out_specs=specs,
        scratch_shapes=list(scratch),
        compiler_params=pltpu.CompilerParams(vmem_limit_bytes=16 << 20),
    )

    def apply(*args):
        return run(
            *[
                a
                if m is None
                else pltpu.with_memory_space_constraint(a, pltpu.VMEM if m is True else pltpu.HBM)
                for a, m in zip(args, ins)
            ]
        )

    return apply


def body(
    component_concentration,
    thermal_level,
    motion_vector,
    component_weight_per_mole,
    collision_size_third,
    potential_depth_volume,
    binary_drag_logpoly,
    specific_warmth_intercept,
    specific_warmth_gradient,
    component_threshold_stress,
):
    species, width, line = component_concentration.shape
    terms = binary_drag_logpoly.shape[0]
    tiles = line // LANES
    units = width * tiles
    rows = species + EXTRA
    per = LANES // (2 * LATERAL_ZONES)
    packs = width // per
    nx, ny = lax.axis_size("gx"), lax.axis_size("gy")
    devices = nx * ny
    conc = component_concentration.reshape(species * width, line)
    motion = motion_vector.reshape(3 * width, line)
    mat_rows = (terms + 2) * species + 16
    count = (species + 4) * width
    keep = True
    field = ((units, rows, LANES), F32, keep)
    mix_scratch = lambda n: [pltpu.VMEM((n * 8, LANES), F32), pltpu.VMEM((5, n, LANES), F32)]
    state, carried, mat, first_x, second_x, first_y, second_y, rate = call(
        mixture_kernel,
        [
            field,
            field,
            ((mat_rows, 2 * species), jnp.bfloat16, keep),
            ((2 * tiles, rows, LANES), F32, keep),
            ((2 * tiles, rows, LANES), F32, keep),
            ((packs, rows, LANES), F32, keep),
            ((packs, rows, LANES), F32, keep),
            ((devices, LANES), F32, pl.ANY),
        ],
        [pl.ANY] * 10,
        [
            pltpu.VMEM((devices, LANES), F32),
            pltpu.VMEM((tiles, count, LANES), F32),
            pltpu.VMEM((1, species), F32),
            pltpu.VMEM((species, species), F32),
            pltpu.VMEM((species, species), F32),
            pltpu.VMEM((terms * species, species), F32),
            pltpu.VMEM((1, species), F32),
            pltpu.VMEM((1, species), F32),
            pltpu.VMEM((1, species), F32),
        ]
        + mix_scratch(units)
        + [pltpu.SemaphoreType.DMA((7,)), pltpu.SemaphoreType.DMA((3 * tiles,))]
        + [pltpu.SemaphoreType.DMA(())],
    )(
        conc,
        thermal_level,
        motion,
        component_weight_per_mole[None],
        collision_size_third,
        potential_depth_volume,
        binary_drag_logpoly.reshape(terms * species, species),
        specific_warmth_intercept[None],
        specific_warmth_gradient[None],
        component_threshold_stress[None],
    )
    top = lax.all_to_all(rate, ("gx", "gy"), 0, 0, tiled=True)
    pair_first = lambda n: [(i, i ^ 1) for i in range(n)]
    pair_second = lambda n: [(i, (i + 1) % n if i % 2 else (i - 1) % n) for i in range(n)]
    inside = [(i, j) for i, j in pair_second(nx) if abs(i - j) == 1]
    got_first_x = lax.ppermute(first_x, "gx", pair_first(nx))
    got_second_x = lax.ppermute(second_x, "gx", inside)
    got_first_y = lax.ppermute(first_y, "gy", pair_first(ny))
    got_second_y = lax.ppermute(second_y, "gy", pair_second(ny))
    batch = 2 if width % 2 == 0 else 1
    weights = jnp.asarray(stencil_weights())
    inner, mat = call(
        functools.partial(inner_kernel, batch, tiles),
        [
            field,
            ((mat_rows, 2 * species), jnp.bfloat16, keep),
        ],
        [keep, keep, pl.ANY, keep],
        [pltpu.VMEM(weights.shape, weights.dtype), pltpu.SemaphoreType.DMA(())],
    )(state, carried, weights, mat)
    halos = 2 * packs + 4 * tiles
    (total,) = call(
        rim_kernel,
        [field],
        [keep] * 3 + [None] * 4 + [keep],
        [
            pltpu.VMEM((halos, rows, LANES), F32),
            pltpu.VMEM((halos, rows, LANES), F32),
        ]
        + mix_scratch(halos)
        + [
            pltpu.VMEM((2 * packs, rows, LANES), F32),
            pltpu.VMEM((8 * packs, rows, LANES), F32),
            pltpu.SemaphoreType.DMA((4,)),
        ],
    )(
        state,
        carried,
        mat,
        got_first_y,
        got_second_y,
        got_first_x,
        got_second_x,
        inner,
    )
    conc_next, temper_next, motion_next, interval = call(
        finish_kernel,
        [
            (conc.shape, F32, pl.ANY),
            (thermal_level.shape, F32, pl.ANY),
            (motion.shape, F32, pl.ANY),
            ((1, 1), F32, pl.ANY),
        ],
        [keep] * 3,
        [
            pltpu.VMEM((tiles, rows * width, LANES), F32),
            pltpu.VMEM((1, 1), F32),
            pltpu.SemaphoreType.DMA((3 * tiles + 1,)),
        ],
    )(state, total, top)
    return (
        conc_next.reshape(component_concentration.shape),
        motion_next.reshape(motion_vector.shape),
        temper_next,
        interval.reshape(()),
    )


def solution(mesh):
    in_specs = (
        P(None, "gx", "gy"),
        P("gx", "gy"),
        P(None, "gx", "gy"),
    ) + (P(),) * 7
    out_specs = (P(None, "gx", "gy"), P(None, "gx", "gy"), P("gx", "gy"), P())
    return jax.shard_map(body, mesh=mesh, in_specs=in_specs, out_specs=out_specs, check_vma=False)
```

```python
import functools

import jax
import jax.numpy as jnp
import numpy as np
from jax import lax
from jax.experimental import pallas as pl
from jax.experimental.pallas import tpu as pltpu
from jax.sharding import PartitionSpec as P


LATERAL_ZONES = 16
CFL_NUMBER = 0.12
GAS_SCALE = 0.01
BETA = 0.7862
LANES = 128
EXTRA = 8
F32 = jnp.float32
VMEM = pltpu.MemorySpace.VMEM


def row_ids():
    return lax.broadcasted_iota(jnp.int32, (EXTRA, LANES), 0)


def split(value):
    high = value.astype(jnp.bfloat16)
    low = (value - high.astype(F32)).astype(jnp.bfloat16)
    return high, low


def fold_rows(value, op):
    parts = [value[8 * i : 8 * i + 8] for i in range(value.shape[0] // 8)]
    while len(parts) > 1:
        half = [op(parts[i], parts[i + 1]) for i in range(0, len(parts) - 1, 2)]
        parts = half + ([parts[-1]] if len(parts) % 2 else [])
    return parts[0]


def column_sum(value):
    return jnp.sum(fold_rows(value, jnp.add), axis=0, keepdims=True)


def write_matrix(mass_ref, size_ref, energy_ref, poly_ref, base_ref, slope_ref, crit_ref, mat_ref):
    species = mass_ref.shape[1]
    terms = poly_ref.shape[0] // species
    inverse = 1.0 / mass_ref[...]
    rows = lax.broadcasted_iota(jnp.int32, (species, species), 0)
    cols = lax.broadcasted_iota(jnp.int32, (species, species), 1)
    same = rows == cols
    column = jnp.sum(
        jnp.where(same, jnp.broadcast_to(inverse, (species, species)), 0.0), axis=1, keepdims=True
    )

    def put(start, block):
        high, low = split(block)
        high, low = high.astype(F32), low.astype(F32)
        mat_ref[start : start + block.shape[0], :] = jnp.concatenate(
            [high, low], axis=1
        ).astype(jnp.bfloat16)

    for k in range(terms):
        block = jnp.where(same, 0.0, poly_ref[k * species : (k + 1) * species, :])
        put(k * species, block * inverse)
    put(terms * species, size_ref[...] * inverse * column)
    put((terms + 1) * species, energy_ref[...] * inverse * column)
    lin = lax.broadcasted_iota(jnp.int32, (16, species), 0)
    block = jnp.where(lin == 0, 1.0, 0.0)
    for k, row in enumerate(
        (inverse, base_ref[...] * inverse, slope_ref[...] * inverse, crit_ref[...] * inverse)
    ):
        block = jnp.where(lin == k + 1, row, block)
    put((terms + 2) * species, block)


def mix_products(units, group, read, mat_ref, lin_ref, resist_ref, extra=None, unit=None, ready=None):
    ids = row_ids()

    def step(j, carry):
        pieces = [read(j, i) for i in range(group)]
        mass = [p[0] for p in pieces]
        species = mass[0].shape[0]
        terms = mat_ref.shape[0] // species - 2
        wide = jnp.concatenate(mass, axis=1)
        high, low = split(wide)
        stacked = jnp.concatenate([high, high, low, low], axis=0)
        both = jnp.concatenate([mat_ref[...], mat_ref[...]], axis=1)
        product = jnp.dot(both, stacked, preferred_element_type=F32)
        for i, (m, temper, *logs) in enumerate(pieces):
            part = product[:, i * LANES : (i + 1) * LANES]
            u = j * group + i if unit is None else unit(j, i)
            logt = logs[0] if logs else jnp.log(temper)
            total = part[(terms - 1) * species : terms * species]
            for k in range(terms - 2, -1, -1):
                total = total * logt + part[k * species : (k + 1) * species]
            resist_ref[u, 0:species, :] = total
            size = column_sum(m * part[terms * species : (terms + 1) * species])
            energy = column_sum(m * part[(terms + 1) * species : (terms + 2) * species])
            lin = part[(terms + 2) * species : (terms + 2) * species + 8]
            lin = jnp.where(ids == 5, size, jnp.where(ids == 6, energy, lin))
            lin = jnp.where(ids == 7, temper, lin)
            row = u * 8 if isinstance(u, int) else pl.multiple_of(u * 8, 8)
            lin_ref[pl.ds(row, 8), :] = lin
            if extra is not None:
                extra(j, i, u, temper, part[(terms + 2) * species : (terms + 2) * species + 1])
        return carry

    if ready is None:
        lax.fori_loop(0, units // group, step, 0)
    else:
        for j in range(units // group):
            ready(j)
            step(j, 0)


def mix_cells(units, lin_ref, plane_ref):
    def plane(k):
        return lin_ref[pl.ds(k, units, stride=8), :]

    density, moles, base, slope, crit, size, energy, temper = [plane(k) for k in range(8)]
    reduced = temper * size / energy
    collision = (
        1.16145 * jnp.exp(-0.14874 * jnp.log(reduced))
        + 0.52487 * jnp.exp(-0.7732 * reduced)
        + 2.16178 * jnp.exp(-2.43787 * reduced)
    )
    inv_moles = 1.0 / moles
    mean_mass = density * inv_moles
    size_mix = size * inv_moles * inv_moles
    viscosity = (
        (40.785 * (0.809 * 0.809))
        * jnp.sqrt(mean_mass * temper)
        / (jnp.exp((2.0 / 3.0) * jnp.log(size_mix)) * collision)
    )
    heat_total = base + slope * temper
    excess = heat_total * inv_moles - 2.5
    ratio = reduced * (1.0 / 1.2593)
    zeta = 2.0 + 10.5 * ratio * ratio
    psi = 1.0 + excess * (0.215 + 0.28288 * excess - 1.061 * BETA + 0.26665 * zeta) / (
        0.6366 + BETA * zeta + (1.061 * BETA) * excess
    )
    conduct = 7.452 * viscosity * psi / mean_mass
    over = GAS_SCALE * temper * moles * moles / crit
    takahashi = 1.0 / (1.0 + 0.25 * over * over)
    front = density * takahashi * jnp.sqrt(temper) * (1.0 / GAS_SCALE)
    inv_density = 1.0 / density
    inv_heat = 1.0 / heat_total
    plane_ref[0] = front
    plane_ref[1] = inv_density
    plane_ref[2] = viscosity
    plane_ref[3] = conduct
    plane_ref[4] = inv_heat
    return jnp.maximum(viscosity * inv_density, conduct * inv_heat)


def coefficient_rows(plane_ref, u):
    ids = row_ids()
    visc = plane_ref[2, pl.ds(u, 1), :]
    cond = plane_ref[3, pl.ds(u, 1), :]
    return jnp.where(ids == 0, cond, jnp.where(ids < 4, visc, 0.0))


def mix_halo(units, group, state_ref, mat_ref, lin_ref, plane_ref, carried_ref):
    species = state_ref.shape[1] - EXTRA

    def read(j, i):
        u = j * group + i
        density = state_ref[u, species + 4 : species + 5, :]
        return state_ref[u, 0:species, :] * density, state_ref[u, species : species + 1, :]

    mix_products(units, group, read, mat_ref, lin_ref, carried_ref)
    mix_cells(units, lin_ref, plane_ref)

    def step(u, carry):
        front = plane_ref[0, pl.ds(u, 1), :]
        fraction = state_ref[u, 0:species, :]
        carried_ref[u, 0:species, :] = front * ((1.0 - fraction) / carried_ref[u, 0:species, :])
        carried_ref[u, species : species + EXTRA, :] = coefficient_rows(plane_ref, u)
        return carry

    lax.fori_loop(0, units, step, 0)


def pack_cells(ref, unit, tiles, start, per):
    reach = LANES // per
    rows = ref.shape[1]
    lanes = lax.broadcasted_iota(jnp.int32, (rows, LANES), 1)
    out = None
    for k in range(per):
        piece = ref[unit + k * tiles]
        turn = (k * reach - start) % LANES
        if turn:
            piece = pltpu.roll(piece, turn, 1)
        out = piece if k == 0 else jnp.where(lanes >= k * reach, piece, out)
    return out


def mixture_kernel(
    conc_hbm, temper_hbm, motion_hbm, mass_hbm, size_hbm, energy_hbm, poly_hbm, base_hbm,
    slope_hbm, crit_hbm,
    state_ref, carried_ref, mat_ref, first_x, second_x, first_y, second_y, rate_hbm,
    rate_ref, base_ref, temper_ref, motion_ref, log_ref, mass_ref, size_ref, energy_ref, poly_ref, heat_ref, slope_ref, crit_ref, lin_ref, plane_ref,
    table_sem, cell_sem, rate_sem,
):
    tiles = base_ref.shape[0]
    width = temper_hbm.shape[0]
    species = mass_ref.shape[1]
    units = tiles * width
    pairs = (
        (mass_hbm, mass_ref), (size_hbm, size_ref), (energy_hbm, energy_ref),
        (poly_hbm, poly_ref), (base_hbm, heat_ref), (slope_hbm, slope_ref), (crit_hbm, crit_ref),
    )
    tables = [
        pltpu.make_async_copy(src, dst, table_sem.at[k]) for k, (src, dst) in enumerate(pairs)
    ]
    copies = [
        pltpu.make_async_copy(
            conc_hbm.at[:, pl.ds(t * LANES, LANES)], base_ref.at[t], cell_sem.at[t]
        )
        for t in range(tiles)
    ]
    for k, (src, dst) in enumerate(((temper_hbm, temper_ref), (motion_hbm, motion_ref))):
        copies.append(pltpu.make_async_copy(src, dst, cell_sem.at[tiles + k]))
    for c in tables + copies:
        c.start()
    for c in tables:
        c.wait()
    write_matrix(
        mass_ref, size_ref, energy_ref, poly_ref, heat_ref, slope_ref, crit_ref, mat_ref
    )
    ids = row_ids()

    def ready(t):
        if t == 0:
            for c in copies:
                c.wait()
            log_ref[...] = jnp.log(temper_ref[...])

    def read(t, x):
        mass = base_ref[t, pl.ds(x, species, stride=width), :]
        ls = slice(t * LANES, (t + 1) * LANES)
        return mass, temper_ref[x : x + 1, ls], log_ref[x : x + 1, ls]

    def extra(t, x, u, temper, density):
        block = jnp.where(ids == 0, temper, jnp.where(ids == 4, density, 0.0))
        for c in range(3):
            at = c * width + x
            row = motion_ref[at : at + 1, t * LANES : (t + 1) * LANES]
            block = jnp.where(ids == c + 1, row, block)
        state_ref[u, species : species + EXTRA, :] = block

    unit = lambda t, x: x * tiles + t
    mix_products(units, width, read, mat_ref, lin_ref, carried_ref, extra, unit, ready)
    rates = mix_cells(units, lin_ref, plane_ref)

    def step(x, best):
        for t in range(tiles):
            u = x * tiles + t
            front = plane_ref[0, pl.ds(u, 1), :]
            inv_density = plane_ref[1, pl.ds(u, 1), :]
            fraction = base_ref[t, pl.ds(x, species, stride=width), :] * inv_density
            share = (1.0 - fraction) / carried_ref[u, 0:species, :]
            state_ref[u, 0:species, :] = fraction
            carried_ref[u, 0:species, :] = front * share
            carried_ref[u, species : species + EXTRA, :] = coefficient_rows(plane_ref, u)
            state_ref[u, species + 5 : species + 6, :] = plane_ref[4, pl.ds(u, 1), :]
            state_ref[u, species + 6 : species + 7, :] = inv_density
            best = jnp.maximum(best, fold_rows(share, jnp.maximum) * (front * inv_density))
        return best

    best = jnp.zeros((8, LANES), F32)
    for x in range(width):
        best = step(x, best)
    top = jnp.maximum(jnp.max(best), jnp.max(rates))
    rate_ref[...] = jnp.full(rate_ref.shape, top, F32)
    send = pltpu.make_async_copy(rate_ref, rate_hbm, rate_sem)
    send.start()

    even_x = lax.rem(lax.axis_index("gx"), 2) == 0
    upper = (width - 2) * tiles
    start_a = jnp.where(even_x, upper, 0)
    start_b = upper - start_a
    for k in range(2 * tiles):
        first_x[k] = state_ref[start_a + k]
        second_x[k] = state_ref[start_b + k]
    even_y = lax.rem(lax.axis_index("gy"), 2) == 0
    reach = 2 * LATERAL_ZONES
    per = LANES // reach
    for g in range(width // per):
        low = pack_cells(state_ref, g * per * tiles, tiles, 0, per)
        high = pack_cells(state_ref, g * per * tiles + tiles - 1, tiles, LANES - reach, per)
        first_y[g] = jnp.where(even_y, high, low)
        second_y[g] = jnp.where(even_y, low, high)
    send.wait()


def weigh(before, here, after, beyond):
    value = 9.0 * (here + after) - (before + beyond)
    slope = 27.0 * (after - here) - (beyond - before)
    return value, slope


def only_value(before, here, after, beyond):
    return 9.0 * (here + after) - (before + beyond)


def z_shift(part, amount):
    zc = LATERAL_ZONES
    z_index = lax.broadcasted_iota(jnp.int32, part.shape, 1) % zc
    near = pltpu.roll(part, (LANES - amount) % LANES, 1)
    far = pltpu.roll(part, (zc - amount) if amount > 0 else LANES - (zc + amount), 1)
    if amount > 0:
        return jnp.where(z_index < zc - amount, near, far)
    return jnp.where(z_index >= -amount, near, far)


def face_weights(offset):
    value = np.select([offset == -1, offset == 0, offset == 1, offset == 2], [-1, 9, 9, -1], 0)
    slope = np.select([offset == -1, offset == 0, offset == 1, offset == 2], [1, -27, 27, -1], 0)
    return value, slope


def stencil_weights():
    zc = LATERAL_ZONES
    src, dst = np.meshgrid(np.arange(LANES), np.arange(LANES), indexing="ij")
    near = (src // zc) == (dst // zc)
    z_value, z_slope = face_weights(np.where(near, (src % zc - dst % zc + 1) % zc - 1, 9))

    def along_y(place):
        gap = place - dst
        return face_weights(np.where(gap % zc == 0, gap // zc, 9))

    y_value, y_slope = along_y(src)
    lent = along_y(np.where(src < 2 * zc, src + LANES, src - LANES))
    blocks = np.concatenate([z_value, y_value, z_slope, y_slope, *lent], axis=1)
    return np.concatenate([blocks, blocks], axis=0).astype(jnp.bfloat16)


def face_flux(f, h, species):
    value, slope = weigh(*f)
    product = only_value(*h) * slope
    drift = column_sum(product[:species]) * 0.0625
    return jnp.concatenate(
        [product[:species] - value[:species] * drift, product[species:]], axis=0
    )


def drifted(product, value, species):
    drift = column_sum(product[:species]) * 0.0625
    return jnp.concatenate([product[:species] - value[:species] * drift, product[species:]], axis=0)


def inner_kernel(
    batch, tiles, state_ref, carried_ref, weight_hbm, mat_ref, rate_ref, mat_out, weight_ref, sem
):
    units, rows, _ = state_ref.shape
    species = rows - EXTRA
    width = units // tiles
    zc = LATERAL_ZONES
    reach = 2 * zc
    wide = lax.broadcasted_iota(jnp.int32, (rows, LANES), 1)
    copy = pltpu.make_async_copy(weight_hbm, weight_ref, sem)
    copy.start()
    mat_out[...] = mat_ref[...]

    def along(t, carry):
        before = None
        for face in range(2, width - 1):
            f = [state_ref[(face + k) * tiles + t] for k in (-2, -1, 0, 1)]
            h = [carried_ref[(face + k) * tiles + t] for k in (-2, -1, 0, 1)]
            flux = face_flux(f, h, species)
            u = (face - 1) * tiles + t
            rate_ref[u] = flux if before is None else flux - before
            before = flux
        u = (width - 2) * tiles + t
        rate_ref[u] = -before
        for x in (0, width - 1):
            rate_ref[x * tiles + t] = jnp.zeros((rows, LANES), F32)
        return carry

    lax.fori_loop(0, tiles, along, 0)
    copy.wait()

    def wings(ref, j):
        own, lent = [], []
        for b in range(batch):
            f = [ref[(j * batch + b) * tiles + t] for t in range(tiles)]
            own += f
            for t in range(tiles):
                lent.append(jnp.where(wide < reach, f[(t + 1) % tiles], f[t - 1]))
        return [jnp.concatenate(split(jnp.concatenate(p, axis=0)), axis=1) for p in (own, lent)]

    def dot(a, start, stop):
        return jnp.dot(a, weight_ref[:, start * LANES : stop * LANES], preferred_element_type=F32)

    def work(j, carry):
        own, lent = wings(state_ref, j)
        first = dot(own, 0, 4)
        second = dot(lent, 4, 6)
        own, lent = wings(carried_ref, j)
        third = dot(own, 0, 2)
        fourth = dot(lent, 4, 5)
        for b in range(batch):
            fluxes = []
            for t in range(tiles):
                u = (j * batch + b) * tiles + t
                i = b * tiles + t
                rs = slice(i * rows, (i + 1) * rows)
                part = lambda m, k: m[rs, k * LANES : (k + 1) * LANES]
                flux = drifted(part(third, 0) * part(first, 2), part(first, 0), species)
                rate_ref[u] = rate_ref[u] + (flux - z_shift(flux, -1))
                value = part(first, 1) + part(second, 0)
                slope = part(first, 3) + part(second, 1)
                flux = drifted((part(third, 1) + part(fourth, 0)) * slope, value, species)
                if t == 0:
                    flux = jnp.where(wide >= zc, flux, 0.0)
                if t == tiles - 1:
                    flux = jnp.where(wide < LANES - reach, flux, 0.0)
                fluxes.append(flux)
            turned = [pltpu.roll(flux, zc, 1) for flux in fluxes]
            for t in range(tiles):
                u = (j * batch + b) * tiles + t
                back = jnp.where(wide >= zc, turned[t], turned[t - 1] if t > 0 else 0.0)
                rate_ref[u] = rate_ref[u] + (fluxes[t] - back)
        return carry

    for j in range(width // batch):
        work(j, 0)


def rim_kernel(
    state_ref, carried_ref, mat_ref, first_y, second_y, first_x, second_x, partial_ref,
    rate_ref,
    halo_ref, halo_carried, lin_ref, plane_ref, edge_ref, pack_ref, halo_sem,
):
    units, rows, _ = state_ref.shape
    species = rows - EXTRA
    packs = first_y.shape[0]
    half = first_x.shape[0]
    tiles = half // 2
    width = units // tiles
    zc = LATERAL_ZONES
    reach = 2 * zc
    per = LANES // reach
    me, peers = lax.axis_index("gx"), lax.axis_size("gx")
    even_x = lax.rem(me, 2) == 0
    even_y = lax.rem(lax.axis_index("gy"), 2) == 0
    at_start, at_end = me == 0, me == peers - 1
    skip = 2 * packs
    low_x, low_y = jnp.where(even_x, half, 0), jnp.where(even_y, packs, 0)
    halos = [
        pltpu.make_async_copy(src, halo_ref.at[pl.ds(start, src.shape[0])], halo_sem.at[k])
        for k, (src, start) in enumerate(
            (
                (first_y, low_y),
                (second_y, packs - low_y),
                (first_x, skip + low_x),
                (second_x, skip + half - low_x),
            )
        )
    ]
    for c in halos:
        c.start()
    for g in range(packs):
        unit = g * per * tiles
        last = unit + tiles - 1
        for k, ref in enumerate((state_ref, carried_ref)):
            for i, (at, start) in enumerate(
                ((unit, 0), (unit, reach), (last, LANES - 2 * reach), (last, LANES - reach))
            ):
                pack_ref[(4 * k + i) * packs + g] = pack_cells(ref, at, tiles, start, per)

    for c in halos:
        c.wait()

    @pl.when(at_start)
    def _():
        for k in range(half):
            halo_ref[skip + k] = state_ref[k % tiles]

    @pl.when(at_end)
    def _():
        for k in range(half):
            halo_ref[skip + half + k] = state_ref[units - tiles + k % tiles]

    total = skip + 2 * half
    group = next(n for n in (8, 6, 4, 3, 2, 1) if total % n == 0)
    mix_halo(total, group, halo_ref, mat_ref, lin_ref, plane_ref, halo_carried)

    ids = row_ids()
    wide = lax.broadcasted_iota(jnp.int32, (rows, LANES), 1)
    lower = wide % reach < zc

    def between(p, q):
        return jnp.where(lower, pltpu.roll(p, LANES - zc, 1), pltpu.roll(q, zc, 1))

    for g in range(packs):
        stencils = []
        for i, halo in enumerate((halo_ref, halo_carried)):
            below, above = halo[g], halo[packs + g]
            low, up, down, high = [pack_ref[(4 * i + k) * packs + g] for k in range(4)]
            stencils.append(
                (
                    (below, between(below, low), low, between(low, up)),
                    (between(down, high), high, between(high, above), above),
                )
            )
        flux = face_flux(stencils[0][0], stencils[1][0], species)
        edge_ref[g] = jnp.where(lower, pltpu.roll(flux, LANES - zc, 1), 0.0) - flux
        flux = face_flux(stencils[0][1], stencils[1][1], species)
        edge_ref[packs + g] = flux - jnp.where(lower, 0.0, pltpu.roll(flux, zc, 1))

    for t in range(tiles):

        def row(inner, outer, x):
            if x < 0:
                return outer[skip + (x + 2) * tiles + t]
            if x >= width:
                return outer[skip + half + (x - width) * tiles + t]
            return inner[x * tiles + t]

        flux = {}
        for face in (0, 1, width - 1, width):
            f = [row(state_ref, halo_ref, face + k) for k in (-2, -1, 0, 1)]
            h = [row(carried_ref, halo_carried, face + k) for k in (-2, -1, 0, 1)]
            flux[face] = face_flux(f, h, species)
        for x in range(width):
            u = x * tiles + t
            g, k = divmod(x, per)
            total = partial_ref[u]
            if x + 1 in flux:
                total = total + flux[x + 1]
            if x in flux:
                total = total - flux[x]
            if t == 0:
                edge = edge_ref[g]
                edge = pltpu.roll(edge, LANES - k * reach, 1) if k else edge
                total = total + jnp.where(wide < reach, edge, 0.0)
            if t == tiles - 1:
                edge = edge_ref[packs + g]
                turn = (LANES - (k + 1) * reach) % LANES
                edge = pltpu.roll(edge, turn, 1) if turn else edge
                total = total + jnp.where(wide >= LANES - reach, edge, 0.0)
            inv_heat = state_ref[u, species + 5 : species + 6, :]
            inv_density = state_ref[u, species + 6 : species + 7, :]
            scale = jnp.where(ids == 0, inv_heat, inv_density)
            total = jnp.concatenate([total[:species], total[species:] * scale], axis=0)
            rate_ref[u] = total


def finish_kernel(
    state_ref, rate_ref, top_ref,
    conc_next, temper_next, motion_next, interval_next,
    next_ref, interval_ref, sem,
):
    tiles, _, _ = next_ref.shape
    units, rows, _ = state_ref.shape
    species = rows - EXTRA
    width = units // tiles
    interval = CFL_NUMBER / jnp.max(top_ref[...], axis=(0, 1), keepdims=True)
    interval_ref[...] = interval
    factor = interval * (1.0 / 384.0)
    outs = [pltpu.make_async_copy(interval_ref, interval_next, sem.at[3 * tiles])]
    outs[0].start()
    for t in range(tiles):
        for x in range(width):
            u = x * tiles + t
            density = state_ref[u, species + 4 : species + 5, :]
            here = jnp.concatenate(
                [state_ref[u, 0:species, :] * density, state_ref[u, species:, :]], axis=0
            )
            next_ref[t, pl.ds(x, rows, stride=width), :] = here + factor * rate_ref[u]
        start = 0
        for k, dst in enumerate((conc_next, temper_next, motion_next)):
            src = next_ref.at[t, pl.ds(start, dst.shape[0])]
            part = dst.at[:, pl.ds(t * LANES, LANES)]
            outs.append(pltpu.make_async_copy(src, part, sem.at[3 * t + k]))
            outs[-1].start()
            start += dst.shape[0]
    for c in outs:
        c.wait()


def call(kernel, outs, ins, scratch=()):
    shapes, specs = [], []
    for shape, dtype, place in outs:
        space = {True: pltpu.VMEM, pl.ANY: pltpu.HBM}.get(place, jax.ShapeDtypeStruct)
        shapes.append(space(shape, dtype))
        specs.append(pl.BlockSpec(memory_space=pl.ANY if place is pl.ANY else VMEM))
    run = pl.pallas_call(
        kernel,
        out_shape=shapes,
        in_specs=[
            pl.BlockSpec(memory_space={True: VMEM, pl.ANY: pltpu.HBM, None: pl.ANY}[m]) for m in ins
        ],
        out_specs=specs,
        scratch_shapes=list(scratch),
        compiler_params=pltpu.CompilerParams(vmem_limit_bytes=16 << 20),
    )

    def apply(*args):
        return run(
            *[
                a
                if m is None
                else pltpu.with_memory_space_constraint(a, pltpu.VMEM if m is True else pltpu.HBM)
                for a, m in zip(args, ins)
            ]
        )

    return apply


def body(
    component_concentration,
    thermal_level,
    motion_vector,
    component_weight_per_mole,
    collision_size_third,
    potential_depth_volume,
    binary_drag_logpoly,
    specific_warmth_intercept,
    specific_warmth_gradient,
    component_threshold_stress,
):
    species, width, line = component_concentration.shape
    terms = binary_drag_logpoly.shape[0]
    tiles = line // LANES
    units = width * tiles
    rows = species + EXTRA
    per = LANES // (2 * LATERAL_ZONES)
    packs = width // per
    nx, ny = lax.axis_size("gx"), lax.axis_size("gy")
    devices = nx * ny
    conc = component_concentration.reshape(species * width, line)
    motion = motion_vector.reshape(3 * width, line)
    mat_rows = (terms + 2) * species + 16
    keep = True
    field = ((units, rows, LANES), F32, keep)
    mix_scratch = lambda n: [pltpu.VMEM((n * 8, LANES), F32), pltpu.VMEM((5, n, LANES), F32)]
    state, carried, mat, first_x, second_x, first_y, second_y, rate = call(
        mixture_kernel,
        [
            field,
            field,
            ((mat_rows, 2 * species), jnp.bfloat16, keep),
            ((2 * tiles, rows, LANES), F32, keep),
            ((2 * tiles, rows, LANES), F32, keep),
            ((packs, rows, LANES), F32, keep),
            ((packs, rows, LANES), F32, keep),
            ((devices, LANES), F32, pl.ANY),
        ],
        [pl.ANY] * 10,
        [
            pltpu.VMEM((devices, LANES), F32),
            pltpu.VMEM((tiles, species * width, LANES), F32),
            pltpu.VMEM((width, line), F32),
            pltpu.VMEM((3 * width, line), F32),
            pltpu.VMEM((width, line), F32),
            pltpu.VMEM((1, species), F32),
            pltpu.VMEM((species, species), F32),
            pltpu.VMEM((species, species), F32),
            pltpu.VMEM((terms * species, species), F32),
            pltpu.VMEM((1, species), F32),
            pltpu.VMEM((1, species), F32),
            pltpu.VMEM((1, species), F32),
        ]
        + mix_scratch(units)
        + [pltpu.SemaphoreType.DMA((7,)), pltpu.SemaphoreType.DMA((tiles + 2,))]
        + [pltpu.SemaphoreType.DMA(())],
    )(
        conc,
        thermal_level,
        motion,
        component_weight_per_mole[None],
        collision_size_third,
        potential_depth_volume,
        binary_drag_logpoly.reshape(terms * species, species),
        specific_warmth_intercept[None],
        specific_warmth_gradient[None],
        component_threshold_stress[None],
    )
    top = lax.all_to_all(rate, ("gx", "gy"), 0, 0, tiled=True)
    pair_first = lambda n: [(i, i ^ 1) for i in range(n)]
    pair_second = lambda n: [(i, (i + 1) % n if i % 2 else (i - 1) % n) for i in range(n)]
    inside = [(i, j) for i, j in pair_second(nx) if abs(i - j) == 1]
    got_first_x = lax.ppermute(first_x, "gx", pair_first(nx))
    got_second_x = lax.ppermute(second_x, "gx", inside)
    got_first_y = lax.ppermute(first_y, "gy", pair_first(ny))
    got_second_y = lax.ppermute(second_y, "gy", pair_second(ny))
    batch = 2 if width % 2 == 0 else 1
    weights = jnp.asarray(stencil_weights())
    inner, mat = call(
        functools.partial(inner_kernel, batch, tiles),
        [
            field,
            ((mat_rows, 2 * species), jnp.bfloat16, keep),
        ],
        [keep, keep, pl.ANY, keep],
        [pltpu.VMEM(weights.shape, weights.dtype), pltpu.SemaphoreType.DMA(())],
    )(state, carried, weights, mat)
    halos = 2 * packs + 4 * tiles
    (total,) = call(
        rim_kernel,
        [field],
        [keep] * 3 + [None] * 4 + [keep],
        [
            pltpu.VMEM((halos, rows, LANES), F32),
            pltpu.VMEM((halos, rows, LANES), F32),
        ]
        + mix_scratch(halos)
        + [
            pltpu.VMEM((2 * packs, rows, LANES), F32),
            pltpu.VMEM((8 * packs, rows, LANES), F32),
            pltpu.SemaphoreType.DMA((4,)),
        ],
    )(
        state,
        carried,
        mat,
        got_first_y,
        got_second_y,
        got_first_x,
        got_second_x,
        inner,
    )
    conc_next, temper_next, motion_next, interval = call(
        finish_kernel,
        [
            (conc.shape, F32, pl.ANY),
            (thermal_level.shape, F32, pl.ANY),
            (motion.shape, F32, pl.ANY),
            ((1, 1), F32, pl.ANY),
        ],
        [keep] * 3,
        [
            pltpu.VMEM((tiles, rows * width, LANES), F32),
            pltpu.VMEM((1, 1), F32),
            pltpu.SemaphoreType.DMA((3 * tiles + 1,)),
        ],
    )(state, total, top)
    return (
        conc_next.reshape(component_concentration.shape),
        motion_next.reshape(motion_vector.shape),
        temper_next,
        interval.reshape(()),
    )


def solution(mesh):
    in_specs = (
        P(None, "gx", "gy"),
        P("gx", "gy"),
        P(None, "gx", "gy"),
    ) + (P(),) * 7
    out_specs = (P(None, "gx", "gy"), P(None, "gx", "gy"), P("gx", "gy"), P())
    return jax.shard_map(body, mesh=mesh, in_specs=in_specs, out_specs=out_specs, check_vma=False)
```

```python
import functools

import jax
import jax.numpy as jnp
import numpy as np
from jax import lax
from jax.experimental import pallas as pl
from jax.experimental.pallas import tpu as pltpu
from jax.sharding import PartitionSpec as P


LATERAL_ZONES = 16
CFL_NUMBER = 0.12
GAS_SCALE = 0.01
BETA = 0.7862
LANES = 128
EXTRA = 8
F32 = jnp.float32
VMEM = pltpu.MemorySpace.VMEM


def row_ids():
    return lax.broadcasted_iota(jnp.int32, (EXTRA, LANES), 0)


def split(value):
    high = value.astype(jnp.bfloat16)
    low = (value - high.astype(F32)).astype(jnp.bfloat16)
    return high, low


def fold_rows(value, op):
    parts = [value[8 * i : 8 * i + 8] for i in range(value.shape[0] // 8)]
    while len(parts) > 1:
        half = [op(parts[i], parts[i + 1]) for i in range(0, len(parts) - 1, 2)]
        parts = half + ([parts[-1]] if len(parts) % 2 else [])
    return parts[0]


def column_sum(value):
    return jnp.sum(fold_rows(value, jnp.add), axis=0, keepdims=True)


def write_matrix(mass_ref, size_ref, energy_ref, poly_ref, base_ref, slope_ref, crit_ref, mat_ref):
    species = mass_ref.shape[1]
    terms = poly_ref.shape[0] // species
    inverse = 1.0 / mass_ref[...]
    rows = lax.broadcasted_iota(jnp.int32, (species, species), 0)
    cols = lax.broadcasted_iota(jnp.int32, (species, species), 1)
    same = rows == cols
    column = jnp.sum(
        jnp.where(same, jnp.broadcast_to(inverse, (species, species)), 0.0), axis=1, keepdims=True
    )

    def put(start, block):
        high, low = split(block)
        high, low = high.astype(F32), low.astype(F32)
        mat_ref[start : start + block.shape[0], :] = jnp.concatenate(
            [high, low], axis=1
        ).astype(jnp.bfloat16)

    for k in range(terms):
        block = jnp.where(same, 0.0, poly_ref[k * species : (k + 1) * species, :])
        put(k * species, block * inverse)
    put(terms * species, size_ref[...] * inverse * column)
    put((terms + 1) * species, energy_ref[...] * inverse * column)
    lin = lax.broadcasted_iota(jnp.int32, (16, species), 0)
    block = jnp.where(lin == 0, 1.0, 0.0)
    for k, row in enumerate(
        (inverse, base_ref[...] * inverse, slope_ref[...] * inverse, crit_ref[...] * inverse)
    ):
        block = jnp.where(lin == k + 1, row, block)
    put((terms + 2) * species, block)


def mix_products(units, group, read, mat_ref, lin_ref, resist_ref, extra=None, unit=None, ready=None):
    ids = row_ids()

    def step(j, carry):
        pieces = [read(j, i) for i in range(group)]
        mass = [p[0] for p in pieces]
        species = mass[0].shape[0]
        terms = mat_ref.shape[0] // species - 2
        wide = jnp.concatenate(mass, axis=1)
        high, low = split(wide)
        stacked = jnp.concatenate([high, high, low, low], axis=0)
        both = jnp.concatenate([mat_ref[...], mat_ref[...]], axis=1)
        product = jnp.dot(both, stacked, preferred_element_type=F32)
        for i, (m, temper, *logs) in enumerate(pieces):
            part = product[:, i * LANES : (i + 1) * LANES]
            u = j * group + i if unit is None else unit(j, i)
            logt = logs[0] if logs else jnp.log(temper)
            total = part[(terms - 1) * species : terms * species]
            for k in range(terms - 2, -1, -1):
                total = total * logt + part[k * species : (k + 1) * species]
            resist_ref[u, 0:species, :] = total
            size = column_sum(m * part[terms * species : (terms + 1) * species])
            energy = column_sum(m * part[(terms + 1) * species : (terms + 2) * species])
            lin = part[(terms + 2) * species : (terms + 2) * species + 8]
            lin = jnp.where(ids == 5, size, jnp.where(ids == 6, energy, lin))
            lin = jnp.where(ids == 7, temper, lin)
            row = u * 8 if isinstance(u, int) else pl.multiple_of(u * 8, 8)
            lin_ref[pl.ds(row, 8), :] = lin
            if extra is not None:
                extra(j, i, u, temper, part[(terms + 2) * species : (terms + 2) * species + 1])
        return carry

    if ready is None:
        lax.fori_loop(0, units // group, step, 0)
    else:
        for j in range(units // group):
            ready(j)
            step(j, 0)


def mix_cells(units, lin_ref, plane_ref):
    def plane(k):
        return lin_ref[pl.ds(k, units, stride=8), :]

    density, moles, base, slope, crit, size, energy, temper = [plane(k) for k in range(8)]
    reduced = temper * size / energy
    collision = (
        1.16145 * jnp.exp(-0.14874 * jnp.log(reduced))
        + 0.52487 * jnp.exp(-0.7732 * reduced)
        + 2.16178 * jnp.exp(-2.43787 * reduced)
    )
    inv_moles = 1.0 / moles
    mean_mass = density * inv_moles
    size_mix = size * inv_moles * inv_moles
    viscosity = (
        (40.785 * (0.809 * 0.809))
        * jnp.sqrt(mean_mass * temper)
        / (jnp.exp((2.0 / 3.0) * jnp.log(size_mix)) * collision)
    )
    heat_total = base + slope * temper
    excess = heat_total * inv_moles - 2.5
    ratio = reduced * (1.0 / 1.2593)
    zeta = 2.0 + 10.5 * ratio * ratio
    psi = 1.0 + excess * (0.215 + 0.28288 * excess - 1.061 * BETA + 0.26665 * zeta) / (
        0.6366 + BETA * zeta + (1.061 * BETA) * excess
    )
    conduct = 7.452 * viscosity * psi / mean_mass
    over = GAS_SCALE * temper * moles * moles / crit
    takahashi = 1.0 / (1.0 + 0.25 * over * over)
    front = density * takahashi * jnp.sqrt(temper) * (1.0 / GAS_SCALE)
    inv_density = 1.0 / density
    inv_heat = 1.0 / heat_total
    plane_ref[0] = front
    plane_ref[1] = inv_density
    plane_ref[2] = viscosity
    plane_ref[3] = conduct
    plane_ref[4] = inv_heat
    return jnp.maximum(viscosity * inv_density, conduct * inv_heat)


def coefficient_rows(plane_ref, u):
    ids = row_ids()
    visc = plane_ref[2, pl.ds(u, 1), :]
    cond = plane_ref[3, pl.ds(u, 1), :]
    return jnp.where(ids == 0, cond, jnp.where(ids < 4, visc, 0.0))


def mix_halo(units, group, state_ref, mat_ref, lin_ref, plane_ref, carried_ref):
    species = state_ref.shape[1] - EXTRA

    def read(j, i):
        u = j * group + i
        density = state_ref[u, species + 4 : species + 5, :]
        return state_ref[u, 0:species, :] * density, state_ref[u, species : species + 1, :]

    mix_products(units, group, read, mat_ref, lin_ref, carried_ref)
    mix_cells(units, lin_ref, plane_ref)

    def step(u, carry):
        front = plane_ref[0, pl.ds(u, 1), :]
        fraction = state_ref[u, 0:species, :]
        carried_ref[u, 0:species, :] = front * ((1.0 - fraction) / carried_ref[u, 0:species, :])
        carried_ref[u, species : species + EXTRA, :] = coefficient_rows(plane_ref, u)
        return carry

    lax.fori_loop(0, units, step, 0)


def pack_cells(ref, unit, tiles, start, per):
    reach = LANES // per
    rows = ref.shape[1]
    lanes = lax.broadcasted_iota(jnp.int32, (rows, LANES), 1)
    out = None
    for k in range(per):
        piece = ref[unit + k * tiles]
        turn = (k * reach - start) % LANES
        if turn:
            piece = pltpu.roll(piece, turn, 1)
        out = piece if k == 0 else jnp.where(lanes >= k * reach, piece, out)
    return out


def mixture_kernel(
    conc_hbm, temper_hbm, motion_hbm, mass_hbm, size_hbm, energy_hbm, poly_hbm, base_hbm,
    slope_hbm, crit_hbm,
    state_ref, carried_ref, mat_ref, first_x, second_x, first_y, second_y, rate_ref,
    base_ref, temper_ref, motion_ref, log_ref, mass_ref, size_ref, energy_ref, poly_ref, heat_ref, slope_ref, crit_ref, lin_ref, plane_ref,
    table_sem, cell_sem,
):
    tiles = base_ref.shape[0]
    width = temper_hbm.shape[0]
    species = mass_ref.shape[1]
    units = tiles * width
    pairs = (
        (mass_hbm, mass_ref), (size_hbm, size_ref), (energy_hbm, energy_ref),
        (poly_hbm, poly_ref), (base_hbm, heat_ref), (slope_hbm, slope_ref), (crit_hbm, crit_ref),
    )
    tables = [
        pltpu.make_async_copy(src, dst, table_sem.at[k]) for k, (src, dst) in enumerate(pairs)
    ]
    copies = [
        pltpu.make_async_copy(
            conc_hbm.at[:, pl.ds(t * LANES, LANES)], base_ref.at[t], cell_sem.at[t]
        )
        for t in range(tiles)
    ]
    for k, (src, dst) in enumerate(((temper_hbm, temper_ref), (motion_hbm, motion_ref))):
        copies.append(pltpu.make_async_copy(src, dst, cell_sem.at[tiles + k]))
    for c in tables + copies:
        c.start()
    for c in tables:
        c.wait()
    write_matrix(
        mass_ref, size_ref, energy_ref, poly_ref, heat_ref, slope_ref, crit_ref, mat_ref
    )
    ids = row_ids()

    def ready(t):
        if t == 0:
            for c in copies:
                c.wait()
            log_ref[...] = jnp.log(temper_ref[...])

    def read(t, x):
        mass = base_ref[t, pl.ds(x, species, stride=width), :]
        ls = slice(t * LANES, (t + 1) * LANES)
        return mass, temper_ref[x : x + 1, ls], log_ref[x : x + 1, ls]

    def extra(t, x, u, temper, density):
        block = jnp.where(ids == 0, temper, jnp.where(ids == 4, density, 0.0))
        for c in range(3):
            at = c * width + x
            row = motion_ref[at : at + 1, t * LANES : (t + 1) * LANES]
            block = jnp.where(ids == c + 1, row, block)
        state_ref[u, species : species + EXTRA, :] = block

    unit = lambda t, x: x * tiles + t
    mix_products(units, width, read, mat_ref, lin_ref, carried_ref, extra, unit, ready)
    rates = mix_cells(units, lin_ref, plane_ref)

    def step(x, best):
        for t in range(tiles):
            u = x * tiles + t
            front = plane_ref[0, pl.ds(u, 1), :]
            inv_density = plane_ref[1, pl.ds(u, 1), :]
            fraction = base_ref[t, pl.ds(x, species, stride=width), :] * inv_density
            share = (1.0 - fraction) / carried_ref[u, 0:species, :]
            state_ref[u, 0:species, :] = fraction
            carried_ref[u, 0:species, :] = front * share
            carried_ref[u, species : species + EXTRA, :] = coefficient_rows(plane_ref, u)
            state_ref[u, species + 5 : species + 6, :] = plane_ref[4, pl.ds(u, 1), :]
            state_ref[u, species + 6 : species + 7, :] = inv_density
            best = jnp.maximum(best, fold_rows(share, jnp.maximum) * (front * inv_density))
        return best

    best = jnp.zeros((8, LANES), F32)
    for x in range(width):
        best = step(x, best)
    top = jnp.maximum(jnp.max(best), jnp.max(rates))
    rate_ref[...] = jnp.full(rate_ref.shape, top, F32)

    even_x = lax.rem(lax.axis_index("gx"), 2) == 0
    upper = (width - 2) * tiles
    start_a = jnp.where(even_x, upper, 0)
    start_b = upper - start_a
    for k in range(2 * tiles):
        first_x[k] = state_ref[start_a + k]
        second_x[k] = state_ref[start_b + k]
    even_y = lax.rem(lax.axis_index("gy"), 2) == 0
    reach = 2 * LATERAL_ZONES
    per = LANES // reach
    for g in range(width // per):
        low = pack_cells(state_ref, g * per * tiles, tiles, 0, per)
        high = pack_cells(state_ref, g * per * tiles + tiles - 1, tiles, LANES - reach, per)
        first_y[g] = jnp.where(even_y, high, low)
        second_y[g] = jnp.where(even_y, low, high)


def weigh(before, here, after, beyond):
    value = 9.0 * (here + after) - (before + beyond)
    slope = 27.0 * (after - here) - (beyond - before)
    return value, slope


def only_value(before, here, after, beyond):
    return 9.0 * (here + after) - (before + beyond)


def z_shift(part, amount):
    zc = LATERAL_ZONES
    z_index = lax.broadcasted_iota(jnp.int32, part.shape, 1) % zc
    near = pltpu.roll(part, (LANES - amount) % LANES, 1)
    far = pltpu.roll(part, (zc - amount) if amount > 0 else LANES - (zc + amount), 1)
    if amount > 0:
        return jnp.where(z_index < zc - amount, near, far)
    return jnp.where(z_index >= -amount, near, far)


def face_weights(offset):
    value = np.select([offset == -1, offset == 0, offset == 1, offset == 2], [-1, 9, 9, -1], 0)
    slope = np.select([offset == -1, offset == 0, offset == 1, offset == 2], [1, -27, 27, -1], 0)
    return value, slope


def stencil_weights():
    zc = LATERAL_ZONES
    src, dst = np.meshgrid(np.arange(LANES), np.arange(LANES), indexing="ij")
    near = (src // zc) == (dst // zc)
    z_value, z_slope = face_weights(np.where(near, (src % zc - dst % zc + 1) % zc - 1, 9))

    def along_y(place):
        gap = place - dst
        return face_weights(np.where(gap % zc == 0, gap // zc, 9))

    y_value, y_slope = along_y(src)
    lent = along_y(np.where(src < 2 * zc, src + LANES, src - LANES))
    blocks = np.concatenate([z_value, y_value, z_slope, y_slope, *lent], axis=1)
    return np.concatenate([blocks, blocks], axis=0).astype(jnp.bfloat16)


def face_flux(f, h, species):
    value, slope = weigh(*f)
    product = only_value(*h) * slope
    drift = column_sum(product[:species]) * 0.0625
    return jnp.concatenate(
        [product[:species] - value[:species] * drift, product[species:]], axis=0
    )


def drifted(product, value, species):
    drift = column_sum(product[:species]) * 0.0625
    return jnp.concatenate([product[:species] - value[:species] * drift, product[species:]], axis=0)


def inner_kernel(
    batch, tiles, state_ref, carried_ref, weight_hbm, mat_ref, rate_ref, mat_out, weight_ref, sem
):
    units, rows, _ = state_ref.shape
    species = rows - EXTRA
    width = units // tiles
    zc = LATERAL_ZONES
    reach = 2 * zc
    wide = lax.broadcasted_iota(jnp.int32, (rows, LANES), 1)
    copy = pltpu.make_async_copy(weight_hbm, weight_ref, sem)
    copy.start()
    mat_out[...] = mat_ref[...]

    def along(t, carry):
        before = None
        for face in range(2, width - 1):
            f = [state_ref[(face + k) * tiles + t] for k in (-2, -1, 0, 1)]
            h = [carried_ref[(face + k) * tiles + t] for k in (-2, -1, 0, 1)]
            flux = face_flux(f, h, species)
            u = (face - 1) * tiles + t
            rate_ref[u] = flux if before is None else flux - before
            before = flux
        u = (width - 2) * tiles + t
        rate_ref[u] = -before
        for x in (0, width - 1):
            rate_ref[x * tiles + t] = jnp.zeros((rows, LANES), F32)
        return carry

    lax.fori_loop(0, tiles, along, 0)
    copy.wait()

    def wings(ref, j):
        own, lent = [], []
        for b in range(batch):
            f = [ref[(j * batch + b) * tiles + t] for t in range(tiles)]
            own += f
            for t in range(tiles):
                lent.append(jnp.where(wide < reach, f[(t + 1) % tiles], f[t - 1]))
        return [jnp.concatenate(split(jnp.concatenate(p, axis=0)), axis=1) for p in (own, lent)]

    def dot(a, start, stop):
        return jnp.dot(a, weight_ref[:, start * LANES : stop * LANES], preferred_element_type=F32)

    def work(j, carry):
        own, lent = wings(state_ref, j)
        first = dot(own, 0, 4)
        second = dot(lent, 4, 6)
        own, lent = wings(carried_ref, j)
        third = dot(own, 0, 2)
        fourth = dot(lent, 4, 5)
        for b in range(batch):
            fluxes = []
            for t in range(tiles):
                u = (j * batch + b) * tiles + t
                i = b * tiles + t
                rs = slice(i * rows, (i + 1) * rows)
                part = lambda m, k: m[rs, k * LANES : (k + 1) * LANES]
                flux = drifted(part(third, 0) * part(first, 2), part(first, 0), species)
                rate_ref[u] = rate_ref[u] + (flux - z_shift(flux, -1))
                value = part(first, 1) + part(second, 0)
                slope = part(first, 3) + part(second, 1)
                flux = drifted((part(third, 1) + part(fourth, 0)) * slope, value, species)
                if t == 0:
                    flux = jnp.where(wide >= zc, flux, 0.0)
                if t == tiles - 1:
                    flux = jnp.where(wide < LANES - reach, flux, 0.0)
                fluxes.append(flux)
            turned = [pltpu.roll(flux, zc, 1) for flux in fluxes]
            for t in range(tiles):
                u = (j * batch + b) * tiles + t
                back = jnp.where(wide >= zc, turned[t], turned[t - 1] if t > 0 else 0.0)
                rate_ref[u] = rate_ref[u] + (fluxes[t] - back)
        return carry

    for j in range(width // batch):
        work(j, 0)


def rim_kernel(
    state_ref, carried_ref, mat_ref, first_y, second_y, first_x, second_x, partial_ref,
    rate_ref,
    halo_ref, halo_carried, lin_ref, plane_ref, edge_ref, pack_ref, halo_sem,
):
    units, rows, _ = state_ref.shape
    species = rows - EXTRA
    packs = first_y.shape[0]
    half = first_x.shape[0]
    tiles = half // 2
    width = units // tiles
    zc = LATERAL_ZONES
    reach = 2 * zc
    per = LANES // reach
    me, peers = lax.axis_index("gx"), lax.axis_size("gx")
    even_x = lax.rem(me, 2) == 0
    even_y = lax.rem(lax.axis_index("gy"), 2) == 0
    at_start, at_end = me == 0, me == peers - 1
    skip = 2 * packs
    low_x, low_y = jnp.where(even_x, half, 0), jnp.where(even_y, packs, 0)
    halos = [
        pltpu.make_async_copy(src, halo_ref.at[pl.ds(start, src.shape[0])], halo_sem.at[k])
        for k, (src, start) in enumerate(
            (
                (first_y, low_y),
                (second_y, packs - low_y),
                (first_x, skip + low_x),
                (second_x, skip + half - low_x),
            )
        )
    ]
    for c in halos:
        c.start()
    for g in range(packs):
        unit = g * per * tiles
        last = unit + tiles - 1
        for k, ref in enumerate((state_ref, carried_ref)):
            for i, (at, start) in enumerate(
                ((unit, 0), (unit, reach), (last, LANES - 2 * reach), (last, LANES - reach))
            ):
                pack_ref[(4 * k + i) * packs + g] = pack_cells(ref, at, tiles, start, per)

    for c in halos:
        c.wait()

    @pl.when(at_start)
    def _():
        for k in range(half):
            halo_ref[skip + k] = state_ref[k % tiles]

    @pl.when(at_end)
    def _():
        for k in range(half):
            halo_ref[skip + half + k] = state_ref[units - tiles + k % tiles]

    total = skip + 2 * half
    group = next(n for n in (8, 6, 4, 3, 2, 1) if total % n == 0)
    mix_halo(total, group, halo_ref, mat_ref, lin_ref, plane_ref, halo_carried)

    ids = row_ids()
    wide = lax.broadcasted_iota(jnp.int32, (rows, LANES), 1)
    lower = wide % reach < zc

    def between(p, q):
        return jnp.where(lower, pltpu.roll(p, LANES - zc, 1), pltpu.roll(q, zc, 1))

    for g in range(packs):
        stencils = []
        for i, halo in enumerate((halo_ref, halo_carried)):
            below, above = halo[g], halo[packs + g]
            low, up, down, high = [pack_ref[(4 * i + k) * packs + g] for k in range(4)]
            stencils.append(
                (
                    (below, between(below, low), low, between(low, up)),
                    (between(down, high), high, between(high, above), above),
                )
            )
        flux = face_flux(stencils[0][0], stencils[1][0], species)
        edge_ref[g] = jnp.where(lower, pltpu.roll(flux, LANES - zc, 1), 0.0) - flux
        flux = face_flux(stencils[0][1], stencils[1][1], species)
        edge_ref[packs + g] = flux - jnp.where(lower, 0.0, pltpu.roll(flux, zc, 1))

    for t in range(tiles):

        def row(inner, outer, x):
            if x < 0:
                return outer[skip + (x + 2) * tiles + t]
            if x >= width:
                return outer[skip + half + (x - width) * tiles + t]
            return inner[x * tiles + t]

        flux = {}
        for face in (0, 1, width - 1, width):
            f = [row(state_ref, halo_ref, face + k) for k in (-2, -1, 0, 1)]
            h = [row(carried_ref, halo_carried, face + k) for k in (-2, -1, 0, 1)]
            flux[face] = face_flux(f, h, species)
        for x in range(width):
            u = x * tiles + t
            g, k = divmod(x, per)
            total = partial_ref[u]
            if x + 1 in flux:
                total = total + flux[x + 1]
            if x in flux:
                total = total - flux[x]
            if t == 0:
                edge = edge_ref[g]
                edge = pltpu.roll(edge, LANES - k * reach, 1) if k else edge
                total = total + jnp.where(wide < reach, edge, 0.0)
            if t == tiles - 1:
                edge = edge_ref[packs + g]
                turn = (LANES - (k + 1) * reach) % LANES
                edge = pltpu.roll(edge, turn, 1) if turn else edge
                total = total + jnp.where(wide >= LANES - reach, edge, 0.0)
            inv_heat = state_ref[u, species + 5 : species + 6, :]
            inv_density = state_ref[u, species + 6 : species + 7, :]
            scale = jnp.where(ids == 0, inv_heat, inv_density)
            total = jnp.concatenate([total[:species], total[species:] * scale], axis=0)
            rate_ref[u] = total


def finish_kernel(
    state_ref, rate_ref, top_ref,
    conc_next, temper_next, motion_next, interval_next,
    next_ref, interval_ref, sem,
):
    tiles, _, _ = next_ref.shape
    units, rows, _ = state_ref.shape
    species = rows - EXTRA
    width = units // tiles
    interval = CFL_NUMBER / jnp.max(top_ref[...], axis=(0, 1), keepdims=True)
    interval_ref[...] = interval
    factor = interval * (1.0 / 384.0)
    outs = [pltpu.make_async_copy(interval_ref, interval_next, sem.at[3 * tiles])]
    outs[0].start()
    for t in range(tiles):
        for x in range(width):
            u = x * tiles + t
            density = state_ref[u, species + 4 : species + 5, :]
            here = jnp.concatenate(
                [state_ref[u, 0:species, :] * density, state_ref[u, species:, :]], axis=0
            )
            next_ref[t, pl.ds(x, rows, stride=width), :] = here + factor * rate_ref[u]
        start = 0
        for k, dst in enumerate((conc_next, temper_next, motion_next)):
            src = next_ref.at[t, pl.ds(start, dst.shape[0])]
            part = dst.at[:, pl.ds(t * LANES, LANES)]
            outs.append(pltpu.make_async_copy(src, part, sem.at[3 * t + k]))
            outs[-1].start()
            start += dst.shape[0]
    for c in outs:
        c.wait()


def call(kernel, outs, ins, scratch=()):
    shapes, specs = [], []
    for shape, dtype, place in outs:
        space = {True: pltpu.VMEM, pl.ANY: pltpu.HBM}.get(place, jax.ShapeDtypeStruct)
        shapes.append(space(shape, dtype))
        specs.append(pl.BlockSpec(memory_space=pl.ANY if place is pl.ANY else VMEM))
    run = pl.pallas_call(
        kernel,
        out_shape=shapes,
        in_specs=[
            pl.BlockSpec(memory_space={True: VMEM, pl.ANY: pltpu.HBM, None: pl.ANY}[m]) for m in ins
        ],
        out_specs=specs,
        scratch_shapes=list(scratch),
        compiler_params=pltpu.CompilerParams(vmem_limit_bytes=16 << 20),
    )

    def apply(*args):
        return run(
            *[
                a
                if m is None
                else pltpu.with_memory_space_constraint(a, pltpu.VMEM if m is True else pltpu.HBM)
                for a, m in zip(args, ins)
            ]
        )

    return apply


def body(
    component_concentration,
    thermal_level,
    motion_vector,
    component_weight_per_mole,
    collision_size_third,
    potential_depth_volume,
    binary_drag_logpoly,
    specific_warmth_intercept,
    specific_warmth_gradient,
    component_threshold_stress,
):
    species, width, line = component_concentration.shape
    terms = binary_drag_logpoly.shape[0]
    tiles = line // LANES
    units = width * tiles
    rows = species + EXTRA
    per = LANES // (2 * LATERAL_ZONES)
    packs = width // per
    nx, ny = lax.axis_size("gx"), lax.axis_size("gy")
    devices = nx * ny
    conc = component_concentration.reshape(species * width, line)
    motion = motion_vector.reshape(3 * width, line)
    mat_rows = (terms + 2) * species + 16
    keep = True
    field = ((units, rows, LANES), F32, keep)
    mix_scratch = lambda n: [pltpu.VMEM((n * 8, LANES), F32), pltpu.VMEM((5, n, LANES), F32)]
    state, carried, mat, first_x, second_x, first_y, second_y, rate = call(
        mixture_kernel,
        [
            field,
            field,
            ((mat_rows, 2 * species), jnp.bfloat16, keep),
            ((2 * tiles, rows, LANES), F32, keep),
            ((2 * tiles, rows, LANES), F32, keep),
            ((packs, rows, LANES), F32, keep),
            ((packs, rows, LANES), F32, keep),
            ((devices, LANES), F32, True),
        ],
        [pl.ANY] * 10,
        [
            pltpu.VMEM((tiles, species * width, LANES), F32),
            pltpu.VMEM((width, line), F32),
            pltpu.VMEM((3 * width, line), F32),
            pltpu.VMEM((width, line), F32),
            pltpu.VMEM((1, species), F32),
            pltpu.VMEM((species, species), F32),
            pltpu.VMEM((species, species), F32),
            pltpu.VMEM((terms * species, species), F32),
            pltpu.VMEM((1, species), F32),
            pltpu.VMEM((1, species), F32),
            pltpu.VMEM((1, species), F32),
        ]
        + mix_scratch(units)
        + [pltpu.SemaphoreType.DMA((7,)), pltpu.SemaphoreType.DMA((tiles + 2,))],
    )(
        conc,
        thermal_level,
        motion,
        component_weight_per_mole[None],
        collision_size_third,
        potential_depth_volume,
        binary_drag_logpoly.reshape(terms * species, species),
        specific_warmth_intercept[None],
        specific_warmth_gradient[None],
        component_threshold_stress[None],
    )
    top = lax.all_to_all(rate, ("gx", "gy"), 0, 0, tiled=True)
    pair_first = lambda n: [(i, i ^ 1) for i in range(n)]
    pair_second = lambda n: [(i, (i + 1) % n if i % 2 else (i - 1) % n) for i in range(n)]
    inside = [(i, j) for i, j in pair_second(nx) if abs(i - j) == 1]
    got_first_x = lax.ppermute(first_x, "gx", pair_first(nx))
    got_second_x = lax.ppermute(second_x, "gx", inside)
    got_first_y = lax.ppermute(first_y, "gy", pair_first(ny))
    got_second_y = lax.ppermute(second_y, "gy", pair_second(ny))
    batch = 2 if width % 2 == 0 else 1
    weights = jnp.asarray(stencil_weights())
    inner, mat = call(
        functools.partial(inner_kernel, batch, tiles),
        [
            field,
            ((mat_rows, 2 * species), jnp.bfloat16, keep),
        ],
        [keep, keep, pl.ANY, keep],
        [pltpu.VMEM(weights.shape, weights.dtype), pltpu.SemaphoreType.DMA(())],
    )(state, carried, weights, mat)
    halos = 2 * packs + 4 * tiles
    (total,) = call(
        rim_kernel,
        [field],
        [keep] * 3 + [None] * 4 + [keep],
        [
            pltpu.VMEM((halos, rows, LANES), F32),
            pltpu.VMEM((halos, rows, LANES), F32),
        ]
        + mix_scratch(halos)
        + [
            pltpu.VMEM((2 * packs, rows, LANES), F32),
            pltpu.VMEM((8 * packs, rows, LANES), F32),
            pltpu.SemaphoreType.DMA((4,)),
        ],
    )(
        state,
        carried,
        mat,
        got_first_y,
        got_second_y,
        got_first_x,
        got_second_x,
        inner,
    )
    conc_next, temper_next, motion_next, interval = call(
        finish_kernel,
        [
            (conc.shape, F32, pl.ANY),
            (thermal_level.shape, F32, pl.ANY),
            (motion.shape, F32, pl.ANY),
            ((1, 1), F32, pl.ANY),
        ],
        [keep] * 3,
        [
            pltpu.VMEM((tiles, rows * width, LANES), F32),
            pltpu.VMEM((1, 1), F32),
            pltpu.SemaphoreType.DMA((3 * tiles + 1,)),
        ],
    )(state, total, top)
    return (
        conc_next.reshape(component_concentration.shape),
        motion_next.reshape(motion_vector.shape),
        temper_next,
        interval.reshape(()),
    )


def solution(mesh):
    in_specs = (
        P(None, "gx", "gy"),
        P("gx", "gy"),
        P(None, "gx", "gy"),
    ) + (P(),) * 7
    out_specs = (P(None, "gx", "gy"), P(None, "gx", "gy"), P("gx", "gy"), P())
    return jax.shard_map(body, mesh=mesh, in_specs=in_specs, out_specs=out_specs, check_vma=False)
```
